128 devices in a mesh: ctx: 16 (over y, z), tp: 8 (over x, core).
Axes of the slice: x: 4, y: 4, z: 4, core: 2. Of those that a mesh axis runs over, the one named last changes fastest.
Arguments:
- queries: bfloat16 [4096, 8192], P('ctx', 'tp'), may hold values from -6 to 6
- new_keys: bfloat16 [4096, 1024], P('ctx', 'tp'), may hold values from -6 to 6
- new_values: bfloat16 [4096, 1024], P('ctx', 'tp'), may hold values from -6 to 6
- positions: int32 [4096], P('ctx'), may hold values from 0 to 262143, as said below
- cache_keys: bfloat16 [32768, 1024], P('ctx', 'tp'), may hold values from -6 to 6
- cache_values: bfloat16 [32768, 1024], P('ctx', 'tp'), may hold values from -6 to 6
- pattern: int32 [64, 4], P('ctx'), may hold values from 0 to 15, all different within a row; in each aligned block of 4 rows (0 to 3, 4 to 7, ...) at most 2 rows name the same one
- out_weight: bfloat16 [8192, 8192], P('tp'), may hold values from -0.0625 to 0.0625
Outputs:
- mixed: bfloat16 [4096, 8192], P(('ctx', 'tp'))
The draws below stay inside these ranges and needn't reach their ends.
Inputs may be any that keep to these rules, and one draw needn't show every extreme that they name: All 4096 positions are distinct. `pattern`: each row names 4 different segments; among the 4 query blocks of one ctx device at most 2 name the same segment, and 2 do in some devices.
All inputs are finite; a program needn't handle non-finite values.
Results may differ from the reference program's by a relative error of at most 0.0075.
Values may be sent and summed in bfloat16 or wider, within the bound.
No kernel may reach another device: no remote copies, remote signals or barrier semaphores. Data moves between devices by JAX's collectives and lax.ppermute only.
A program may use at most 128 MiB of HBM per device.

```python
import math
import jax
import jax.numpy as jnp
import numpy as np
from jax import lax

D = 8192
H = 64
KVH = 8
HD = 128
QB = 64
TOPB = 4
CAP = 2
SPAN = 262144
QB_DEV = 4
KV_DEV = 2048
NQB = 64
QTOK = 4096
CTXLEN = 32768
N_CTX = 16


def spread_positions(key):
    base_key = jax.random.fold_in(key, 7)
    order = jax.random.permutation(jax.random.fold_in(base_key, 1), QTOK).astype(jnp.int32)
    stride = SPAN // QTOK
    jitter = jax.random.randint(jax.random.fold_in(base_key, 2), (QTOK,), 0, stride, dtype=jnp.int32)
    jitter = jnp.where(order == 0, 0, jnp.where(order == QTOK - 1, stride - 1, jitter))
    return (order * stride + jitter).astype(jnp.int32)


def draw_positions(key, part):
    return spread_positions(key)


def draw_queries(key, part):
    own_key = jax.random.fold_in(key, 21)
    return jnp.clip(1.5 * jax.random.normal(own_key, (QTOK, H * HD), jnp.float32), -6.0, 6.0).astype(jnp.bfloat16)


def draw_new_keys(key, part):
    own_key = jax.random.fold_in(key, 22)
    return jnp.clip(jax.random.normal(own_key, (QTOK, KVH * HD), jnp.float32), -6.0, 6.0).astype(jnp.bfloat16)


def draw_cache_keys(key, part):
    own_key = jax.random.fold_in(key, 23)
    return jnp.clip(jax.random.normal(own_key, (CTXLEN, KVH * HD), jnp.float32), -6.0, 6.0).astype(jnp.bfloat16)


def block_levels(key, dims, pieces, smallest, top_value):
    def one(dim, shards_of):
        steps = jax.random.uniform(jax.random.fold_in(jax.random.fold_in(key, 6), dim), (shards_of,), jnp.float32, smallest / len(pieces), top_value / len(pieces))
        return jnp.repeat(jnp.exp(steps), dims[dim] // shards_of).reshape((-1,) + (1,) * (len(dims) - dim - 1))

    loudness = one(*pieces[0])
    for cut in pieces[1:]:
        loudness = loudness * one(*cut)
    return loudness


def routed_block(key, own, number, rows, number_of, top, most, skew):
    ranking = jax.random.permutation(key, number_of)
    heavy_load, common = portions_of(number_of, rows * top, most, skew, True), portions_of(number_of, rows * top, most, skew, False)
    places = jnp.arange(number_of)

    def named(sizes, rotation):
        used = int((sizes > 0).sum())
        fixed = max(1, used // 4)
        passed = fixed + (places - fixed + rotation * (used - fixed)) % max(1, number_of - fixed)
        return jnp.zeros((number_of,), jnp.int32).at[ranking[jnp.where(places < fixed, places, passed)]].set(jnp.asarray(sizes, jnp.int32))

    sizes = jnp.where(number % 4 == 0, named(heavy_load, number // 4), named(common, number - number // 4 - 1))
    mixed = jax.random.permutation(jax.random.fold_in(own, 3), number_of)
    source_of, sink = mixed[0:number_of // 2 * 2:2], mixed[1:number_of // 2 * 2:2]
    margin = jnp.minimum(sizes[source_of] - 1, most - sizes[sink]) // 2
    margin = jnp.where((source_of == ranking[0]) | (sink == ranking[0]) | (sizes[sink] == 0), 0, jnp.maximum(margin, 0))
    passed = jax.random.randint(jax.random.fold_in(own, 4), (number_of // 2,), 0, 1 << 20) % (margin + 1)
    sizes = sizes.at[source_of].add(-passed).at[sink].add(passed)
    labels = jnp.searchsorted(jnp.cumsum(sizes), jnp.arange(rows * top), side="right").astype(jnp.int32)
    grid = labels.reshape(top, rows).T
    grid = grid[jax.random.permutation(jax.random.fold_in(own, 1), rows)]
    rotation = jax.random.randint(jax.random.fold_in(own, 2), (rows, 1), 0, top)
    return jnp.take_along_axis(grid, (jnp.arange(top)[None, :] + rotation) % top, axis=1)


def portions_of(number_of, total, limit, slope, full):
    loads = [(1 << 20) // math.isqrt(rank ** slope) + 1 for rank in range(1, number_of + 1)]
    largest = limit if full else min(limit, max(-(-total // number_of), total * loads[0] // sum(loads)))
    least = 1 if total - largest >= number_of - 1 else 0
    counts, spare = [largest] + [least] * (number_of - 1), total - largest - least * (number_of - 1)
    while spare > 0:
        movable = [i for i in range(1, number_of) if counts[i] < largest] or [i for i in range(1, number_of) if counts[i] < limit]
        whole, remaining = sum([loads[i] for i in movable]), spare
        for i in movable:
            addition = min(limit - counts[i], max(1, remaining * loads[i] // whole), spare)
            counts[i] = counts[i] + addition
            spare = spare - addition
    return np.array(counts)


def gaussian(key, shape, width, most, pieces=(), held_as=jnp.bfloat16):
    factor_of = block_levels(key, shape, pieces, -0.22, 0.18) if pieces else 1.0
    result = jax.random.normal(key, shape, jnp.float32) * width * factor_of
    return jnp.minimum(jnp.maximum(result, -most), most).astype(held_as)


def setup_inputs(seed: int = 0) -> dict:
    splits = jax.random.split(jax.random.key(seed), 9)
    queries = draw_queries(jax.random.fold_in(splits[8], 71), 0)
    new_keys = draw_new_keys(jax.random.fold_in(splits[8], 71), 0)
    new_values = gaussian(splits[2], (QTOK, KVH * HD), 1.0, 6.0, ((0, 16), (1, 8)))
    positions = draw_positions(jax.random.fold_in(splits[8], 71), 0)
    cache_keys = draw_cache_keys(jax.random.fold_in(splits[8], 71), 0)
    cache_values = gaussian(splits[5], (CTXLEN, KVH * HD), 1.0, 6.0, ((0, 16), (1, 8)))
    pattern_keys = jax.random.split(jax.random.fold_in(splits[6], 1), NQB // QB_DEV)
    pattern_turns = jax.random.permutation(jax.random.fold_in(splits[6], 3), NQB // QB_DEV)
    pattern = jax.vmap(lambda own, number: routed_block(jax.random.fold_in(splits[6], 2), own, number, QB_DEV, N_CTX, TOPB, CAP, 2))(pattern_keys, pattern_turns).reshape((NQB, TOPB))
    out_weight = gaussian(splits[7], (H * HD, D), (H * HD) ** -0.5, 0.0625, ((0, 8),))
    return {"queries": queries, "new_keys": new_keys, "new_values": new_values, "positions": positions, "cache_keys": cache_keys, "cache_values": cache_values, "pattern": pattern, "out_weight": out_weight}


NEG_FILL = -1e+30

def reference(queries, new_keys, new_values, positions, cache_keys, cache_values, pattern, out_weight):
    group_size = H // KVH
    scaling = 1.0 / math.sqrt(HD)
    segment_keys = cache_keys.reshape(N_CTX, KV_DEV, KVH, HD)
    segment_values = cache_values.reshape(N_CTX, KV_DEV, KVH, HD)
    fresh_keys = new_keys.reshape(QTOK, KVH, HD).astype(jnp.float32)
    fresh_values = new_values.reshape(QTOK, KVH, HD).astype(jnp.float32)
    block_positions = positions.reshape(NQB, QB)

    def one_block(inputs):
        block_queries, block_pattern, query_positions = inputs
        query_float = block_queries.reshape(QB, KVH, group_size, HD).astype(jnp.float32)

        def one_segment(segment):
            seg_keys = lax.dynamic_index_in_dim(segment_keys, segment, 0, keepdims=False).astype(jnp.float32)
            seg_values = lax.dynamic_index_in_dim(segment_values, segment, 0, keepdims=False).astype(jnp.float32)
            scores = jnp.einsum('tgrd,sgd->tgrs', query_float, seg_keys) * scaling
            largest = lax.optimization_barrier(jnp.max(scores, axis=-1))
            weights = jnp.exp(scores - largest[..., None])
            totals = lax.optimization_barrier(jnp.sum(weights, axis=-1))
            rounded = lax.optimization_barrier(weights.astype(jnp.bfloat16)).astype(jnp.float32)
            mixed_values = jnp.einsum('tgrs,sgd->tgrd', rounded, seg_values) / totals[..., None]
            return (mixed_values, largest + jnp.log(totals))
        part_out, part_log = lax.map(one_segment, block_pattern)
        scores = jnp.einsum('tgrd,sgd->tgrs', query_float, fresh_keys) * scaling
        visible = (positions[None, :] <= query_positions[:, None])[:, None, None, :]
        masked = jnp.where(visible, scores, NEG_FILL)
        largest = lax.optimization_barrier(jnp.max(masked, axis=-1))
        weights = jnp.where(visible, jnp.exp(masked - largest[..., None]), 0.0)
        totals = lax.optimization_barrier(jnp.sum(weights, axis=-1))
        rounded = lax.optimization_barrier(weights.astype(jnp.bfloat16)).astype(jnp.float32)
        fresh_out = jnp.einsum('tgrs,sgd->tgrd', rounded, fresh_values) / totals[..., None]
        fresh_log = largest + jnp.log(totals)
        all_log = jnp.concatenate([part_log, fresh_log[None]], axis=0)
        all_out = jnp.concatenate([part_out, fresh_out[None]], axis=0)
        top_log = lax.optimization_barrier(jnp.max(all_log, axis=0))
        log_total = top_log + jnp.log(lax.optimization_barrier(jnp.sum(jnp.exp(all_log - top_log[None]), axis=0)))
        shares = jnp.exp(all_log - log_total[None])
        attended = lax.optimization_barrier(jnp.sum(shares[..., None] * all_out, axis=0))
        return attended.reshape(QB, H * HD).astype(jnp.bfloat16)
    attention = lax.map(one_block, (queries.reshape(NQB, QB, H * HD), pattern, block_positions))
    attention = attention.reshape(QTOK, H * HD)
    return jnp.dot(attention, out_weight, preferred_element_type=jnp.float32).astype(jnp.bfloat16)
```

```python
import functools
import math

import jax
import jax.numpy as jnp
from jax import lax
from jax.experimental import pallas as pl
from jax.experimental.pallas import tpu as pltpu
from jax.sharding import PartitionSpec as P

HD = 128
GROUP = 8
SIDE = 4
XN = 4
QB = 64
ROWS = QB * GROUP
SEG = 2048
NEW = 256
QW = GROUP * HD
META = 16
KV_ROWS = 2 * (SEG + NEW) + META
V_AT = SEG + NEW
RET_W = QW + 128
BASE = 64
NEG = -1e30
SCALE = 1.0 / math.sqrt(HD)
TO_EXP2 = SCALE * math.log2(math.e)
BF = jnp.bfloat16
F32 = jnp.float32
AXES = ("ctx", "tp")


def pairs(kind, shift):
    out = []
    for y in range(SIDE):
        for z in range(SIDE):
            for x in range(XN):
                for c in range(2):
                    to = [y, z, x, c]
                    if kind == "c":
                        to[3] = 1 - c
                    elif kind == "x":
                        to[2] = (x + shift) % XN
                    else:
                        along = (0 if c == 0 else 1) if kind == "k" else (1 if c == 0 else 0)
                        to[along] = (to[along] + shift) % SIDE
                    src = (y * SIDE + z) * 2 * XN + x * 2 + c
                    dst = (to[0] * SIDE + to[1]) * 2 * XN + to[2] * 2 + to[3]
                    out.append((src, dst))
    return out


def move(value, kind, shift):
    return lax.ppermute(value, AXES, pairs(kind, shift))


def digits(positions):
    p = positions.astype(jnp.int32)
    return jnp.stack([p // (BASE * BASE), (p // BASE) % BASE, p % BASE]).astype(BF)


def undigits(parts):
    f = parts.astype(F32)
    return f[0] * (BASE * BASE) + f[1] * BASE + f[2]


def dot_t(a, b):
    return lax.dot_general(a, b, (((1,), (1,)), ((), ())), preferred_element_type=F32)


def attend_kernel(
    n_home, n_kv, resume, final, flags, *refs
):
    refs = list(refs)
    q_refs = [refs.pop(0) for _ in range(n_home)]
    kv_refs = [refs.pop(0) for _ in range(n_kv)]
    qpos_ref = refs.pop(0)
    kpos_ref = refs.pop(0)
    if resume:
        acc_in, ml_in = refs.pop(0), refs.pop(0)
    if final:
        outs = [refs.pop(0) for _ in range(n_home)]
    else:
        acc_out, ml_out = refs.pop(0), refs.pop(0)
    kv_scr, q_scr, m_scr, acc_scr, sems = refs
    b = pl.program_id(0)
    blocks = NEW // QB

    def fetch(j):
        return pltpu.make_async_copy(kv_refs[j], kv_scr.at[j], sems.at[j])

    @pl.when(b == 0)
    def _():
        for j in range(n_kv):
            fetch(j).start()

    for home in range(n_home):

        @pl.when(b // blocks == home)
        def _(home=home):
            at = pl.multiple_of((b % blocks) * QB, QB)
            for h in range(GROUP):
                q_scr[h * QB : (h + 1) * QB, :] = q_refs[home][
                    pl.ds(at, QB), h * HD : (h + 1) * HD
                ]

    if resume:
        ml = ml_in[...]
        m_scr[...] = jnp.broadcast_to(ml[:, :1], (ROWS, HD))
        acc_scr[:, :HD] = acc_in[...]
        acc_scr[:, HD:] = jnp.broadcast_to(ml[:, HD - 1 :], (ROWS, HD))
    else:
        m_scr[...] = jnp.full((ROWS, HD), NEG, F32)
        acc_scr[...] = jnp.zeros((ROWS, 2 * HD), F32)

    @pl.when(b == 0)
    def _():
        for j in range(n_kv):
            fetch(j).wait()

    step_rows = 256
    step_keys = 512

    def update(j, first, count, width, mask):
        for i in range(ROWS // step_rows):
            rows = slice(i * step_rows, (i + 1) * step_rows)
            q = q_scr[rows, :]
            m = m_scr[rows, :1]
            acc = acc_scr[rows, :]
            for n in range(count):
                k = kv_scr[j, first + n * width : first + (n + 1) * width, :]
                v = kv_scr[j, V_AT + first + n * width : V_AT + first + (n + 1) * width, :]
                s = dot_t(q, k)
                if mask is not None:
                    s = jnp.where(mask, s, NEG)
                top = jnp.maximum(m, jnp.max(s, axis=1, keepdims=True))
                p = jnp.exp2((s - top) * TO_EXP2)
                wide = jnp.concatenate([v, jnp.ones((width, HD), BF)], axis=1)
                acc = acc * jnp.exp2((m - top) * TO_EXP2) + jnp.dot(
                    p.astype(BF), wide, preferred_element_type=F32
                )
                m = top
            m_scr[rows, :] = jnp.broadcast_to(m, (step_rows, HD))
            acc_scr[rows, :] = acc

    def one_slot(j, carry):
        qp = qpos_ref[...]
        qp = jnp.concatenate([qp, qp], axis=1)
        qp = jnp.concatenate([qp] * (step_rows // QB), axis=0)
        update(j, SEG, 1, NEW, kpos_ref[j] <= qp)

        @pl.when(flags[b * n_kv + j] > 0)
        def _():
            update(j, 0, SEG // step_keys, step_keys, None)

        return carry

    if n_kv == 1:
        one_slot(0, 0)
    else:
        lax.fori_loop(0, n_kv, one_slot, 0)

    if not final:
        acc_out[...] = acc_scr[:, :HD]
        lane = lax.broadcasted_iota(jnp.int32, (ROWS, HD), 1)
        ml_out[...] = jnp.where(lane < HD // 2, m_scr[...], acc_scr[:, HD:])
        return
    total = acc_scr[:, HD:]
    out = acc_scr[:, :HD] / total
    log = m_scr[...] * SCALE + jnp.log(total)
    hi = log.astype(BF).astype(F32)
    mid = (log - hi).astype(BF).astype(F32)
    low = log - hi - mid
    lane = lax.broadcasted_iota(jnp.int32, (QB, HD), 1)
    logs = jnp.zeros((QB, HD), F32)
    for h in range(GROUP):
        rows = slice(h * QB, (h + 1) * QB)
        for n, part in enumerate((hi, mid, low)):
            logs = jnp.where(lane == n * GROUP + h, part[rows], logs)
    for home in range(n_home):

        @pl.when(b // blocks == home)
        def _(home=home):
            for h in range(GROUP):
                outs[home][:, h * HD : (h + 1) * HD] = out[h * QB : (h + 1) * QB].astype(BF)
            outs[home][:, QW:] = logs.astype(BF)


def attend(name, flags, q_list, kv_list, qpos, kpos, state=None, final=False):
    n_home, n_kv = len(q_list), len(kv_list)
    blocks = NEW // QB
    steps = n_home * blocks
    whole = lambda shape: pl.BlockSpec(shape, lambda b, f: (0,) * len(shape))
    tile = pl.BlockSpec((ROWS, HD), lambda b, f: (b, 0))
    in_specs = (
        [whole((NEW + META, QW))] * n_home
        + [pl.BlockSpec(memory_space=pl.ANY)] * n_kv
        + [pl.BlockSpec((QB, HD), lambda b, f: (b, 0)), whole((n_kv, 1, NEW))]
    )
    args = list(q_list) + list(kv_list) + [qpos, kpos]
    if state is not None:
        in_specs += [tile, tile]
        args += list(state)
    if final:
        out_shape = [jax.ShapeDtypeStruct((NEW, RET_W), BF)] * n_home
        out_specs = [
            pl.BlockSpec(
                (QB, RET_W),
                lambda b, f, home=home: (jnp.clip(b - home * blocks, 0, blocks - 1), 0),
            )
            for home in range(n_home)
        ]
    else:
        out_shape = [jax.ShapeDtypeStruct((steps * ROWS, HD), F32)] * 2
        out_specs = [tile, tile]
    work = steps * n_kv * ROWS * (SEG // 4 + NEW)
    return pl.pallas_call(
        functools.partial(attend_kernel, n_home, n_kv, state is not None, final),
        name=name,
        out_shape=out_shape,
        grid_spec=pltpu.PrefetchScalarGridSpec(
            num_scalar_prefetch=1,
            grid=(steps,),
            in_specs=in_specs,
            out_specs=out_specs,
            scratch_shapes=[
                pltpu.VMEM((n_kv, KV_ROWS, HD), BF),
                pltpu.VMEM((ROWS, HD), BF),
                pltpu.VMEM((ROWS, HD), F32),
                pltpu.VMEM((ROWS, 2 * HD), F32),
                pltpu.SemaphoreType.DMA((n_kv,)),
            ],
        ),
        compiler_params=pltpu.CompilerParams(vmem_limit_bytes=40 << 20),
        cost_estimate=pl.CostEstimate(
            flops=work * HD * 4 * 2, bytes_accessed=steps * ROWS * HD * 8, transcendentals=work
        ),
    )(flags, *args)


def project_kernel(n_parts, core, *refs):
    parts = refs[:n_parts]
    w_ref, keep_ref, send_ref, att_scr = refs[n_parts:]

    @pl.when(pl.program_id(0) == 0)
    def _():
        for t in range(NEW // 32):
            rows = slice(t * 32, (t + 1) * 32)
            logs = []
            for part in parts:
                packed = part[rows, QW:].astype(F32)
                logs.append(
                    packed[:, :GROUP]
                    + packed[:, GROUP : 2 * GROUP]
                    + packed[:, 2 * GROUP : 3 * GROUP]
                )
            top = functools.reduce(jnp.maximum, logs)
            shares = [jnp.exp(log - top) for log in logs]
            total = functools.reduce(jnp.add, shares)
            shares = [share / total for share in shares]
            away = jnp.where(core[0] == t % 2, 0, NEW // 2)
            at = pl.multiple_of(away + (t // 2) * 32, 32)
            for h in range(GROUP):
                mixed = functools.reduce(
                    jnp.add,
                    [
                        share[:, h : h + 1] * part[rows, h * HD : (h + 1) * HD].astype(F32)
                        for share, part in zip(shares, parts)
                    ],
                )
                att_scr[pl.ds(at, 32), h * HD : (h + 1) * HD] = mixed.astype(BF)

    result = jnp.dot(att_scr[...], w_ref[...], preferred_element_type=F32).astype(BF)
    keep_ref[...] = result[: NEW // 2]
    send_ref[...] = result[NEW // 2 :]


def project(core, parts, weight):
    width = weight.shape[1]
    tile = 1024
    half = pl.BlockSpec((NEW // 2, tile), lambda n, c: (0, n))
    return pl.pallas_call(
        functools.partial(project_kernel, len(parts)),
        name="project",
        out_shape=[jax.ShapeDtypeStruct((NEW // 2, width), BF)] * 2,
        grid_spec=pltpu.PrefetchScalarGridSpec(
            num_scalar_prefetch=1,
            grid=(width // tile,),
            in_specs=[pl.BlockSpec((NEW, RET_W), lambda n, c: (0, 0))] * len(parts)
            + [pl.BlockSpec((QW, tile), lambda n, c: (0, n))],
            out_specs=[half, half],
            scratch_shapes=[pltpu.VMEM((NEW, QW), BF)],
        ),
        compiler_params=pltpu.CompilerParams(vmem_limit_bytes=24 << 20),
        cost_estimate=pl.CostEstimate(
            flops=2 * NEW * QW * width,
            bytes_accessed=QW * width * 2 + NEW * width * 2,
            transcendentals=0,
        ),
    )(core, *parts, weight)


def per_device(
    queries, new_keys, new_values, positions, cache_keys, cache_values, pattern, out_weight
):
    ctx = lax.axis_index("ctx")
    tp = lax.axis_index("tp")
    core = tp % 2
    x = tp // 2
    y, z = ctx // SIDE, ctx % SIDE

    own_digits = digits(positions)
    q_meta = jnp.concatenate([own_digits.reshape(-1), pattern.reshape(-1).astype(BF)])
    q_meta = jnp.pad(q_meta, (0, META * QW - q_meta.shape[0])).reshape(META, QW)
    k_meta = jnp.pad(own_digits.reshape(-1, HD), ((0, META - 3 * NEW // HD), (0, 0)))
    q_own = jnp.concatenate([queries, q_meta], axis=0)
    kv_own = jnp.concatenate([cache_keys, new_keys, cache_values, new_values, k_meta], axis=0)

    q_at = {0: q_own}
    kv_at = {0: kv_own}
    for shift in (1, 3):
        q_at[-shift % SIDE] = move(q_own, "q", shift)
    for shift in (1, 3):
        kv_at[-shift % SIDE] = move(kv_own, "k", shift)
    q_at[2] = move(q_own, "q", 2)
    kv_at[2] = move(kv_own, "k", 2)

    def segment_at(offset):
        along_y = ((y + offset) % SIDE) * SIDE + z
        along_z = y * SIDE + (z + offset) % SIDE
        return jnp.where(core == 0, along_y, along_z)

    def patterns_at(offset):
        row = q_at[offset][NEW]
        return row[3 * NEW : 3 * NEW + 16].astype(F32).astype(jnp.int32).reshape(4, 4)

    def flags_of(q_offsets, kv_offsets):
        rows = jnp.concatenate([patterns_at(o) for o in q_offsets], axis=0)
        segments = jnp.stack([segment_at(o) for o in kv_offsets])
        hits = jnp.any(rows[:, None, :] == segments[None, :, None], axis=-1)
        return hits.astype(jnp.int32).reshape(-1)

    def qpos_of(q_offsets):
        found = [undigits(q_at[o][NEW, : 3 * NEW].reshape(3, NEW)) for o in q_offsets]
        return jnp.broadcast_to(jnp.concatenate(found)[:, None], (NEW * len(found), HD))

    def kpos_of(kv_offsets):
        rows = slice(KV_ROWS - META, KV_ROWS - META + 3 * NEW // HD)
        return jnp.stack([undigits(kv_at[o][rows].reshape(3, NEW))[None] for o in kv_offsets])

    def run(name, q_offsets, kv_offsets, state=None, final=False):
        return attend(
            name,
            flags_of(q_offsets, kv_offsets),
            [q_at[o] for o in q_offsets],
            [kv_at[o] for o in kv_offsets],
            qpos_of(q_offsets),
            kpos_of(kv_offsets),
            state,
            final,
        )

    away = (1, 3, 2)
    own_state = run("own", (0,), (0,))
    state = run("near", away, (0,))
    state = run("sides", away, (1, 3), state)
    returns = run("far", away, (2,), state, True)
    received = [move(part, "q", offset) for offset, part in zip(away, returns)]
    (mine,) = run("home", (0,), (1, 3, 2), own_state, True)

    keep, send = project(core.reshape(1), [mine] + received, out_weight)
    other = move(send, "c", 0)

    def group(shift):
        at = ((x + shift) % XN) * 32
        return lax.dynamic_slice_in_dim(keep, at, 32, 0).astype(F32) + lax.dynamic_slice_in_dim(
            other, at, 32, 0
        ).astype(F32)

    arrived = [move(group(shift).astype(BF), "x", shift) for shift in (1, 3, 2)]
    result = group(0)
    for part in arrived:
        result = result + part.astype(F32)
    return result.astype(BF)


def solution(mesh):
    placed = (
        P("ctx", "tp"),
        P("ctx", "tp"),
        P("ctx", "tp"),
        P("ctx"),
        P("ctx", "tp"),
        P("ctx", "tp"),
        P("ctx", None),
        P("tp", None),
    )
    return jax.shard_map(
        per_device, mesh=mesh, in_specs=placed, out_specs=P(("ctx", "tp"), None), check_vma=False
    )
```

```python
import functools
import math

import jax
import jax.numpy as jnp
from jax import lax
from jax.experimental import pallas as pl
from jax.experimental.pallas import tpu as pltpu
from jax.sharding import PartitionSpec as P

HD = 128
GROUP = 8
SIDE = 4
XN = 4
QB = 64
STEP_ROWS = 256
STEP_KEYS = 512
SEG = 2048
NEW = 256
QW = GROUP * HD
META = 16
KV_ROWS = 2 * (SEG + NEW) + META
V_AT = SEG + NEW
RET_W = QW + 128
BASE = 64
NEG = -1e30
SCALE = 1.0 / math.sqrt(HD)
TO_EXP2 = SCALE * math.log2(math.e)
BF = jnp.bfloat16
F32 = jnp.float32
AXES = ("ctx", "tp")


def pairs(kind, shift):
    out = []
    for y in range(SIDE):
        for z in range(SIDE):
            for x in range(XN):
                for c in range(2):
                    to = [y, z, x, c]
                    if kind == "c":
                        to[3] = 1 - c
                    elif kind == "x":
                        to[2] = (x + shift) % XN
                    else:
                        along = (0 if c == 0 else 1) if kind == "k" else (1 if c == 0 else 0)
                        to[along] = (to[along] + shift) % SIDE
                    src = (y * SIDE + z) * 2 * XN + x * 2 + c
                    dst = (to[0] * SIDE + to[1]) * 2 * XN + to[2] * 2 + to[3]
                    out.append((src, dst))
    return out


def move(value, kind, shift):
    return lax.ppermute(value, AXES, pairs(kind, shift))


def digits(positions):
    p = positions.astype(jnp.int32)
    return jnp.stack([p // (BASE * BASE), (p // BASE) % BASE, p % BASE]).astype(BF)


def undigits(parts):
    f = parts.astype(F32)
    return f[0] * (BASE * BASE) + f[1] * BASE + f[2]


def dot_t(a, b):
    return lax.dot_general(a, b, (((1,), (1,)), ((), ())), preferred_element_type=F32)


def attend_kernel(n_home, n_kv, tokens, resume, final, flags, *refs):
    refs = list(refs)
    q_refs = [refs.pop(0) for _ in range(n_home)]
    kv_refs = [refs.pop(0) for _ in range(n_kv)]
    qpos_ref = refs.pop(0)
    kpos_ref = refs.pop(0)
    if resume:
        acc_in, ml_in = refs.pop(0), refs.pop(0)
    if final:
        outs = [refs.pop(0) for _ in range(n_home)]
    else:
        acc_out, ml_out = refs.pop(0), refs.pop(0)
    k_scr, v_scr, q_scr, m_scr, acc_scr, sems = refs
    home_id = pl.program_id(0)
    blocks = tokens // QB

    def fetch(j):
        return (
            pltpu.make_async_copy(kv_refs[j].at[pl.ds(0, V_AT)], k_scr.at[j], sems.at[j, 0]),
            pltpu.make_async_copy(
                kv_refs[j].at[pl.ds(V_AT, V_AT)], v_scr.at[j, :, pl.ds(0, HD)], sems.at[j, 1]
            ),
        )

    @pl.when(home_id == 0)
    def _():
        for j in range(n_kv):
            for copy in fetch(j):
                copy.start()
        for j in range(n_kv):
            v_scr[j, :, HD:] = jnp.ones((V_AT, HD), BF)

    if n_home == 1:
        q_src = q_refs[0]
    else:
        q_src = q_scr
        for home in range(n_home):

            @pl.when(home_id == home)
            def _(home=home):
                q_scr[...] = q_refs[home][...]

    for h in range(GROUP):
        cols = slice(h * HD, (h + 1) * HD)
        if resume:
            m_scr[:, cols] = jnp.broadcast_to(ml_in[:, h : h + 1], (tokens, HD))
            acc_scr[:, h * 2 * HD : h * 2 * HD + HD] = acc_in[:, cols]
            acc_scr[:, h * 2 * HD + HD : (h + 1) * 2 * HD] = jnp.broadcast_to(
                ml_in[:, GROUP + h : GROUP + h + 1], (tokens, HD)
            )
        else:
            m_scr[:, cols] = jnp.full((tokens, HD), NEG, F32)
            acc_scr[:, h * 2 * HD : (h + 1) * 2 * HD] = jnp.zeros((tokens, 2 * HD), F32)

    @pl.when(home_id == 0)
    def _():
        for j in range(n_kv):
            for copy in fetch(j):
                copy.wait()

    def advance(q, m, acc, k, v, mask):
        s = dot_t(q, k)
        if mask is not None:
            s = jnp.where(mask, s, NEG)
        peak = jnp.broadcast_to(jnp.max(s, axis=1, keepdims=True), m.shape)
        top = jnp.maximum(m, peak)
        p = jnp.exp2((s - jnp.concatenate([top] * (s.shape[1] // HD), axis=1)) * TO_EXP2)
        decay = jnp.exp2((m - top) * TO_EXP2)
        acc = acc * jnp.concatenate([decay, decay], axis=1) + jnp.dot(
            p.astype(BF), v, preferred_element_type=F32
        )
        return top, acc

    def fresh(j, carry):
        qp = qpos_ref[...]
        mask = kpos_ref[j] <= jnp.concatenate([qp, qp], axis=1)
        k = k_scr[j, SEG:, :]
        v = v_scr[j, SEG:, :]
        for h in range(GROUP):
            cols = slice(h * HD, (h + 1) * HD)
            wide = slice(h * 2 * HD, (h + 1) * 2 * HD)
            top, acc = advance(q_src[:, cols], m_scr[:, cols], acc_scr[:, wide], k, v, mask)
            m_scr[:, cols] = top
            acc_scr[:, wide] = acc
        return carry

    per_pass = STEP_ROWS // QB

    def cached(item, carry):
        j, block = item // blocks, item % blocks

        @pl.when(flags[(home_id * n_kv + j) * blocks + block] > 0)
        def _():
            rows = pl.ds(pl.multiple_of(block * QB, QB), QB)
            for first in range(0, GROUP, per_pass):
                heads = range(first, first + per_pass)
                q = jnp.concatenate([q_src[rows, h * HD : (h + 1) * HD] for h in heads], axis=0)
                m = jnp.concatenate([m_scr[rows, h * HD : (h + 1) * HD] for h in heads], axis=0)
                acc = jnp.concatenate(
                    [acc_scr[rows, h * 2 * HD : (h + 1) * 2 * HD] for h in heads], axis=0
                )
                for n in range(SEG // STEP_KEYS):
                    keys = slice(n * STEP_KEYS, (n + 1) * STEP_KEYS)
                    m, acc = advance(q, m, acc, k_scr[j, keys, :], v_scr[j, keys, :], None)
                for n, h in enumerate(heads):
                    part = slice(n * QB, (n + 1) * QB)
                    m_scr[rows, h * HD : (h + 1) * HD] = m[part]
                    acc_scr[rows, h * 2 * HD : (h + 1) * 2 * HD] = acc[part]

        return carry

    if n_kv == 1:
        fresh(0, 0)
    else:
        lax.fori_loop(0, n_kv, fresh, 0)
    lax.fori_loop(0, n_kv * blocks, cached, 0)

    lane = lax.broadcasted_iota(jnp.int32, (tokens, HD), 1)
    if not final:
        ml = jnp.zeros((tokens, HD), F32)
        for h in range(GROUP):
            acc_out[:, h * HD : (h + 1) * HD] = acc_scr[:, h * 2 * HD : h * 2 * HD + HD]
            ml = jnp.where(lane == h, m_scr[:, h * HD : (h + 1) * HD], ml)
            ml = jnp.where(lane == GROUP + h, acc_scr[:, h * 2 * HD + HD : (h + 1) * 2 * HD], ml)
        ml_out[...] = ml
        return

    def emit(out):
        logs = jnp.zeros((tokens, HD), F32)
        for h in range(GROUP):
            cols = slice(h * HD, (h + 1) * HD)
            total = acc_scr[:, h * 2 * HD + HD : (h + 1) * 2 * HD]
            out[:, cols] = (acc_scr[:, h * 2 * HD : h * 2 * HD + HD] / total).astype(BF)
            log = m_scr[:, cols] * SCALE + jnp.log(total)
            logs = jnp.where(lax.rem(lane, GROUP) == h, log, logs)
        hi = logs.astype(BF).astype(F32)
        mid = (logs - hi).astype(BF).astype(F32)
        parts = jnp.where(lane < GROUP, hi, jnp.where(lane < 2 * GROUP, mid, logs - hi - mid))
        out[:, QW:] = parts.astype(BF)

    for home in range(n_home):
        if n_home == 1:
            emit(outs[0])
        else:
            pl.when(home_id == home)(functools.partial(emit, outs[home]))


def attend(name, flags, q_list, kv_list, qpos, kpos, state=None, final=False, tokens=NEW, part=0):
    n_home, n_kv = len(q_list), len(kv_list)
    fixed = lambda shape, at=(0, 0, 0): pl.BlockSpec(shape, lambda i, f: at[: len(shape)])
    span = NEW // tokens
    state_span = 1 if state is None else state[0].shape[0] // (n_home * tokens)
    in_specs = (
        [fixed((tokens, QW), (part, 0))] * n_home
        + [pl.BlockSpec(memory_space=pl.ANY)] * n_kv
        + [
            pl.BlockSpec((tokens, HD), lambda i, f: (i * span + part, 0)),
            fixed((n_kv, 1, NEW)),
        ]
    )
    args = list(q_list) + list(kv_list) + [qpos, kpos]
    if state is not None:
        at = lambda i, f: (i * state_span + (part if state_span > 1 else 0), 0)
        in_specs += [pl.BlockSpec((tokens, QW), at), pl.BlockSpec((tokens, HD), at)]
        args += list(state)
    if final:
        out_shape = [jax.ShapeDtypeStruct((tokens, RET_W), BF)] * n_home
        out_specs = [fixed((tokens, RET_W))] * n_home
    else:
        out_shape = [
            jax.ShapeDtypeStruct((n_home * tokens, QW), F32),
            jax.ShapeDtypeStruct((n_home * tokens, HD), F32),
        ]
        out_specs = [
            pl.BlockSpec((tokens, QW), lambda i, f: (i, 0)),
            pl.BlockSpec((tokens, HD), lambda i, f: (i, 0)),
        ]
    work = n_home * n_kv * tokens * GROUP * (SEG // 4 + NEW)
    return pl.pallas_call(
        functools.partial(attend_kernel, n_home, n_kv, tokens, state is not None, final),
        name=name,
        out_shape=out_shape,
        grid_spec=pltpu.PrefetchScalarGridSpec(
            num_scalar_prefetch=1,
            grid=(n_home,),
            in_specs=in_specs,
            out_specs=out_specs,
            scratch_shapes=[
                pltpu.VMEM((n_kv, V_AT, HD), BF),
                pltpu.VMEM((n_kv, V_AT, 2 * HD), BF),
                pltpu.VMEM((tokens, QW), BF),
                pltpu.VMEM((tokens, QW), F32),
                pltpu.VMEM((tokens, 2 * QW), F32),
                pltpu.SemaphoreType.DMA((n_kv, 2)),
            ],
        ),
        compiler_params=pltpu.CompilerParams(vmem_limit_bytes=36 << 20),
        cost_estimate=pl.CostEstimate(
            flops=work * HD * 4 * 2,
            bytes_accessed=n_home * tokens * QW * 8,
            transcendentals=work,
        ),
    )(flags, *args)


def project_kernel(n_parts, core, *refs):
    parts = refs[:n_parts]
    w_ref, keep_ref, send_ref, att_scr = refs[n_parts:]

    @pl.when(pl.program_id(0) == 0)
    def _():
        for t in range(NEW // 32):
            rows = slice(t * 32, (t + 1) * 32)
            logs = []
            for part in parts:
                packed = part[rows, QW:].astype(F32)
                logs.append(
                    packed[:, :GROUP]
                    + packed[:, GROUP : 2 * GROUP]
                    + packed[:, 2 * GROUP : 3 * GROUP]
                )
            top = functools.reduce(jnp.maximum, logs)
            shares = [jnp.exp(log - top) for log in logs]
            total = functools.reduce(jnp.add, shares)
            shares = [share / total for share in shares]
            away = jnp.where(core[0] == t % 2, 0, NEW // 2)
            at = pl.multiple_of(away + (t // 2) * 32, 32)
            for h in range(GROUP):
                mixed = functools.reduce(
                    jnp.add,
                    [
                        share[:, h : h + 1] * part[rows, h * HD : (h + 1) * HD].astype(F32)
                        for share, part in zip(shares, parts)
                    ],
                )
                att_scr[pl.ds(at, 32), h * HD : (h + 1) * HD] = mixed.astype(BF)

    result = jnp.dot(att_scr[...], w_ref[...], preferred_element_type=F32).astype(BF)
    keep_ref[...] = result[: NEW // 2]
    send_ref[...] = result[NEW // 2 :]


def project(core, parts, weight):
    width = weight.shape[1]
    tile = 1024
    half = pl.BlockSpec((NEW // 2, tile), lambda n, c: (0, n))
    return pl.pallas_call(
        functools.partial(project_kernel, len(parts)),
        name="project",
        out_shape=[jax.ShapeDtypeStruct((NEW // 2, width), BF)] * 2,
        grid_spec=pltpu.PrefetchScalarGridSpec(
            num_scalar_prefetch=1,
            grid=(width // tile,),
            in_specs=[pl.BlockSpec((NEW, RET_W), lambda n, c: (0, 0))] * len(parts)
            + [pl.BlockSpec((QW, tile), lambda n, c: (0, n))],
            out_specs=[half, half],
            scratch_shapes=[pltpu.VMEM((NEW, QW), BF)],
        ),
        compiler_params=pltpu.CompilerParams(vmem_limit_bytes=24 << 20),
        cost_estimate=pl.CostEstimate(
            flops=2 * NEW * QW * width,
            bytes_accessed=QW * width * 2 + NEW * width * 2,
            transcendentals=0,
        ),
    )(core, *parts, weight)


def per_device(
    queries, new_keys, new_values, positions, cache_keys, cache_values, pattern, out_weight
):
    ctx = lax.axis_index("ctx")
    tp = lax.axis_index("tp")
    core = tp % 2
    x = tp // 2
    y, z = ctx // SIDE, ctx % SIDE

    own_digits = digits(positions)
    q_meta = jnp.concatenate([own_digits.reshape(-1), pattern.reshape(-1).astype(BF)])
    q_meta = jnp.pad(q_meta, (0, META * QW - q_meta.shape[0])).reshape(META, QW)
    k_meta = jnp.pad(own_digits.reshape(-1, HD), ((0, META - 3 * NEW // HD), (0, 0)))
    q_own = jnp.concatenate([queries, q_meta], axis=0)
    kv_own = jnp.concatenate([cache_keys, new_keys, cache_values, new_values, k_meta], axis=0)

    q_at = {0: q_own}
    kv_at = {0: kv_own}
    for shift in (1, 3):
        q_at[-shift % SIDE] = move(q_own, "q", shift)
    for shift in (1, 3):
        kv_at[-shift % SIDE] = move(kv_own, "k", shift)
    q_at[2] = move(q_own, "q", 2)
    kv_at[2] = move(kv_own, "k", 2)

    def segment_at(offset):
        along_y = ((y + offset) % SIDE) * SIDE + z
        along_z = y * SIDE + (z + offset) % SIDE
        return jnp.where(core == 0, along_y, along_z)

    def patterns_at(offset):
        row = q_at[offset][NEW]
        return row[3 * NEW : 3 * NEW + 16].astype(F32).astype(jnp.int32).reshape(4, 4)

    def flags_of(q_offsets, kv_offsets):
        rows = jnp.stack([patterns_at(o) for o in q_offsets])
        segments = jnp.stack([segment_at(o) for o in kv_offsets])
        hits = jnp.any(rows[:, None] == segments[None, :, None, None], axis=-1)
        return hits.astype(jnp.int32).reshape(-1)

    def qpos_of(q_offsets):
        found = [undigits(q_at[o][NEW, : 3 * NEW].reshape(3, NEW)) for o in q_offsets]
        return jnp.broadcast_to(jnp.concatenate(found)[:, None], (NEW * len(found), HD))

    def kpos_of(kv_offsets):
        rows = slice(KV_ROWS - META, KV_ROWS - META + 3 * NEW // HD)
        return jnp.stack([undigits(kv_at[o][rows].reshape(3, NEW))[None] for o in kv_offsets])

    def run(name, q_offsets, kv_offsets, state=None, final=False):
        return attend(
            name,
            flags_of(q_offsets, kv_offsets),
            [q_at[o] for o in q_offsets],
            [kv_at[o] for o in kv_offsets],
            qpos_of(q_offsets),
            kpos_of(kv_offsets),
            state,
            final,
        )

    away = (1, 3, 2)
    own_state = run("own", (0,), (0,))
    state = run("near", away, (0,))
    state = run("sides", away, (1, 3), state)
    returns = run("far", away, (2,), state, True)
    received = [move(part, "q", offset) for offset, part in zip(away, returns)]
    (mine,) = run("home", (0,), (1, 3, 2), own_state, True)

    keep, send = project(core.reshape(1), [mine] + received, out_weight)
    other = move(send, "c", 0)

    def group(shift):
        at = ((x + shift) % XN) * 32
        return lax.dynamic_slice_in_dim(keep, at, 32, 0).astype(F32) + lax.dynamic_slice_in_dim(
            other, at, 32, 0
        ).astype(F32)

    arrived = [move(group(shift).astype(BF), "x", shift) for shift in (1, 3, 2)]
    result = group(0)
    for part in arrived:
        result = result + part.astype(F32)
    return result.astype(BF)


def solution(mesh):
    placed = (
        P("ctx", "tp"),
        P("ctx", "tp"),
        P("ctx", "tp"),
        P("ctx"),
        P("ctx", "tp"),
        P("ctx", "tp"),
        P("ctx", None),
        P("tp", None),
    )
    return jax.shard_map(
        per_device, mesh=mesh, in_specs=placed, out_specs=P(("ctx", "tp"), None), check_vma=False
    )
```

```python
import functools
import math

import jax
import jax.numpy as jnp
from jax import lax
from jax.experimental import pallas as pl
from jax.experimental.pallas import tpu as pltpu
from jax.sharding import PartitionSpec as P


HD = 128
GROUP = 8
SIDE = 4
XN = 4
QB = 64
HALF = 128
PIECE = 16
STEP_KEYS = 512
SEG = 2048
NEW = 256
QW = GROUP * HD
META = 16
KV_ROWS = 2 * (SEG + NEW) + META
V_AT = SEG + NEW
RET_W = QW + 128
BASE = 64
NEG = -1e30
SCALE = 1.0 / math.sqrt(HD)
TO_EXP2 = SCALE * math.log2(math.e)
BF = jnp.bfloat16
F32 = jnp.float32
AXES = ("ctx", "tp")


def pairs(kind, shift):
    out = []
    for y in range(SIDE):
        for z in range(SIDE):
            for x in range(XN):
                for c in range(2):
                    to = [y, z, x, c]
                    if kind == "c":
                        to[3] = 1 - c
                    elif kind == "x":
                        to[2] = (x + shift) % XN
                    else:
                        along = (0 if c == 0 else 1) if kind == "k" else (1 if c == 0 else 0)
                        to[along] = (to[along] + shift) % SIDE
                    src = (y * SIDE + z) * 2 * XN + x * 2 + c
                    dst = (to[0] * SIDE + to[1]) * 2 * XN + to[2] * 2 + to[3]
                    out.append((src, dst))
    return out


def move(value, kind, shift):
    return lax.ppermute(value, AXES, pairs(kind, shift))


def digits(positions):
    p = positions.astype(jnp.int32)
    return jnp.stack([p // (BASE * BASE), (p // BASE) % BASE, p % BASE]).astype(BF)


def undigits(parts):
    f = parts.astype(F32)
    return f[0] * (BASE * BASE) + f[1] * BASE + f[2]


def dot_t(a, b):
    return lax.dot_general(a, b, (((1,), (1,)), ((), ())), preferred_element_type=F32)


def attend_kernel(n_home, n_kv, tokens, resume, final, flags, *refs):
    refs = list(refs)
    q_refs = [refs.pop(0) for _ in range(n_home)]
    kv_refs = [refs.pop(0) for _ in range(n_kv)]
    qpos_ref = refs.pop(0)
    kpos_ref = refs.pop(0)
    if resume:
        acc_in, ml_in = refs.pop(0), refs.pop(0)
    if final:
        outs = [refs.pop(0) for _ in range(n_home)]
    else:
        acc_out, ml_out = refs.pop(0), refs.pop(0)
    k_scr, v_scr, q_scr, m_scr, acc_scr, sems = refs
    home_id = pl.program_id(0)
    blocks = NEW // QB

    def fetch(j):
        return (
            pltpu.make_async_copy(kv_refs[j].at[pl.ds(0, V_AT)], k_scr.at[j], sems.at[j, 0]),
            pltpu.make_async_copy(
                kv_refs[j].at[pl.ds(V_AT, V_AT)], v_scr.at[j, :, pl.ds(0, HD)], sems.at[j, 1]
            ),
        )

    @pl.when(home_id == 0)
    def _():
        for j in range(n_kv):
            for copy in fetch(j):
                copy.start()
        for j in range(n_kv):
            v_scr[j, :, HD:] = jnp.ones((V_AT, HD), BF)

    if n_home == 1:
        q_src = q_refs[0]
    else:
        q_src = q_scr
        for home in range(n_home):

            @pl.when(home_id == home)
            def _(home=home):
                q_scr[...] = q_refs[home][...]

    for h in range(GROUP):
        cols = slice(h * HD, (h + 1) * HD)
        if resume:
            m_scr[:, cols] = jnp.broadcast_to(ml_in[:, h : h + 1], (tokens, HD))
            acc_scr[:, h * 2 * HD : h * 2 * HD + HD] = acc_in[:, cols]
            acc_scr[:, h * 2 * HD + HD : (h + 1) * 2 * HD] = jnp.broadcast_to(
                ml_in[:, GROUP + h : GROUP + h + 1], (tokens, HD)
            )
        else:
            m_scr[:, cols] = jnp.full((tokens, HD), NEG, F32)
            acc_scr[:, h * 2 * HD : (h + 1) * 2 * HD] = jnp.zeros((tokens, 2 * HD), F32)

    @pl.when(home_id == 0)
    def _():
        for j in range(n_kv):
            for copy in fetch(j):
                copy.wait()

    def advance(q, m, acc, k, v, mask):
        s = dot_t(q, k)
        if mask is not None:
            s = jnp.where(mask, s, NEG)
        peak = jnp.broadcast_to(jnp.max(s, axis=1, keepdims=True), m.shape)
        top = jnp.maximum(m, peak)
        p = jnp.exp2((s - jnp.concatenate([top] * (s.shape[1] // HD), axis=1)) * TO_EXP2)
        decay = jnp.exp2((m - top) * TO_EXP2)
        acc = acc * jnp.concatenate([decay, decay], axis=1) + jnp.dot(
            p.astype(BF), v, preferred_element_type=F32
        )
        return top, acc

    def fresh(j, carry):
        qp = qpos_ref[...]
        mask = kpos_ref[j] <= jnp.concatenate([qp, qp], axis=1)
        k = k_scr[j, SEG:, :]
        v = v_scr[j, SEG:, :]
        for h in range(GROUP):
            cols = slice(h * HD, (h + 1) * HD)
            wide = slice(h * 2 * HD, (h + 1) * 2 * HD)
            top, acc = advance(q_src[:, cols], m_scr[:, cols], acc_scr[:, wide], k, v, mask)
            m_scr[:, cols] = top
            acc_scr[:, wide] = acc
        return carry

    short = HALF // blocks

    def cached(item, carry):
        j, block = item // blocks, item % blocks

        @pl.when(flags[(home_id * n_kv + j) * blocks + block] > 0)
        def _():
            for half in range(tokens // HALF):
                rows = pl.ds(pl.multiple_of(half * HALF + block * short, short), short)
                heads = range(GROUP)
                q = jnp.concatenate([q_src[rows, h * HD : (h + 1) * HD] for h in heads], axis=0)
                m = jnp.concatenate([m_scr[rows, h * HD : (h + 1) * HD] for h in heads], axis=0)
                acc = jnp.concatenate(
                    [acc_scr[rows, h * 2 * HD : (h + 1) * 2 * HD] for h in heads], axis=0
                )
                for n in range(SEG // STEP_KEYS):
                    keys = slice(n * STEP_KEYS, (n + 1) * STEP_KEYS)
                    m, acc = advance(q, m, acc, k_scr[j, keys, :], v_scr[j, keys, :], None)
                for h in heads:
                    part = slice(h * short, (h + 1) * short)
                    m_scr[rows, h * HD : (h + 1) * HD] = m[part]
                    acc_scr[rows, h * 2 * HD : (h + 1) * 2 * HD] = acc[part]

        return carry

    if n_kv == 1:
        fresh(0, 0)
    else:
        lax.fori_loop(0, n_kv, fresh, 0)
    lax.fori_loop(0, n_kv * blocks, cached, 0)

    lane = lax.broadcasted_iota(jnp.int32, (tokens, HD), 1)
    if not final:
        ml = jnp.zeros((tokens, HD), F32)
        for h in range(GROUP):
            acc_out[:, h * HD : (h + 1) * HD] = acc_scr[:, h * 2 * HD : h * 2 * HD + HD]
            ml = jnp.where(lane == h, m_scr[:, h * HD : (h + 1) * HD], ml)
            ml = jnp.where(lane == GROUP + h, acc_scr[:, h * 2 * HD + HD : (h + 1) * 2 * HD], ml)
        ml_out[...] = ml
        return

    def emit(out):
        logs = jnp.zeros((tokens, HD), F32)
        for h in range(GROUP):
            cols = slice(h * HD, (h + 1) * HD)
            total = acc_scr[:, h * 2 * HD + HD : (h + 1) * 2 * HD]
            out[:, cols] = (acc_scr[:, h * 2 * HD : h * 2 * HD + HD] / total).astype(BF)
            log = m_scr[:, cols] * SCALE + jnp.log(total)
            logs = jnp.where(lax.rem(lane, GROUP) == h, log, logs)
        hi = logs.astype(BF).astype(F32)
        mid = (logs - hi).astype(BF).astype(F32)
        parts = jnp.where(lane < GROUP, hi, jnp.where(lane < 2 * GROUP, mid, logs - hi - mid))
        out[:, QW:] = parts.astype(BF)

    for home in range(n_home):
        if n_home == 1:
            emit(outs[0])
        else:
            pl.when(home_id == home)(functools.partial(emit, outs[home]))


def attend(flags, q_list, kv_list, qpos, kpos, state=None, final=False, tokens=NEW, part=0):
    n_home, n_kv = len(q_list), len(kv_list)
    fixed = lambda shape, at=(0, 0, 0): pl.BlockSpec(shape, lambda i, f: at[: len(shape)])
    span = NEW // tokens
    state_span = 1 if state is None else state[0].shape[0] // (n_home * tokens)
    in_specs = (
        [fixed((tokens, QW), (part, 0))] * n_home
        + [pl.BlockSpec(memory_space=pl.ANY)] * n_kv
        + [
            pl.BlockSpec((tokens, HD), lambda i, f: (i * span + part, 0)),
            fixed((n_kv, 1, NEW)),
        ]
    )
    args = list(q_list) + list(kv_list) + [qpos, kpos]
    if state is not None:
        at = lambda i, f: (i * state_span + (part if state_span > 1 else 0), 0)
        in_specs += [pl.BlockSpec((tokens, QW), at), pl.BlockSpec((tokens, HD), at)]
        args += list(state)
    if final:
        out_shape = [jax.ShapeDtypeStruct((tokens, RET_W), BF)] * n_home
        out_specs = [fixed((tokens, RET_W))] * n_home
    else:
        out_shape = [
            jax.ShapeDtypeStruct((n_home * tokens, QW), F32),
            jax.ShapeDtypeStruct((n_home * tokens, HD), F32),
        ]
        out_specs = [
            pl.BlockSpec((tokens, QW), lambda i, f: (i, 0)),
            pl.BlockSpec((tokens, HD), lambda i, f: (i, 0)),
        ]
    work = n_home * n_kv * tokens * GROUP * (SEG // 4 + NEW)
    return pl.pallas_call(
        functools.partial(attend_kernel, n_home, n_kv, tokens, state is not None, final),
        out_shape=out_shape,
        grid_spec=pltpu.PrefetchScalarGridSpec(
            num_scalar_prefetch=1,
            grid=(n_home,),
            in_specs=in_specs,
            out_specs=out_specs,
            scratch_shapes=[
                pltpu.VMEM((n_kv, V_AT, HD), BF),
                pltpu.VMEM((n_kv, V_AT, 2 * HD), BF),
                pltpu.VMEM((tokens, QW), BF),
                pltpu.VMEM((tokens, QW), F32),
                pltpu.VMEM((tokens, 2 * QW), F32),
                pltpu.SemaphoreType.DMA((n_kv, 2)),
            ],
        ),
        compiler_params=pltpu.CompilerParams(vmem_limit_bytes=36 << 20),
        cost_estimate=pl.CostEstimate(
            flops=work * HD * 4 * 2,
            bytes_accessed=n_home * tokens * QW * 8,
            transcendentals=work,
        ),
    )(flags, *args)


def project_kernel(n_parts, core, *refs):
    parts = refs[:n_parts]
    w_ref, keep_ref, send_ref, att_scr = refs[n_parts:]

    @pl.when(pl.program_id(0) == 0)
    def _():
        for t in range(HALF // PIECE):
            rows = slice(t * PIECE, (t + 1) * PIECE)
            logs = []
            for part in parts:
                packed = part[rows, QW:].astype(F32)
                logs.append(
                    packed[:, :GROUP]
                    + packed[:, GROUP : 2 * GROUP]
                    + packed[:, 2 * GROUP : 3 * GROUP]
                )
            top = functools.reduce(jnp.maximum, logs)
            shares = [jnp.exp(log - top) for log in logs]
            total = functools.reduce(jnp.add, shares)
            shares = [share / total for share in shares]
            away = jnp.where(core[0] == t % 2, 0, HALF // 2)
            at = pl.multiple_of(away + (t // 2) * PIECE, PIECE)
            for h in range(GROUP):
                mixed = functools.reduce(
                    jnp.add,
                    [
                        share[:, h : h + 1] * part[rows, h * HD : (h + 1) * HD].astype(F32)
                        for share, part in zip(shares, parts)
                    ],
                )
                att_scr[pl.ds(at, PIECE), h * HD : (h + 1) * HD] = mixed.astype(BF)

    result = jnp.dot(att_scr[...], w_ref[...], preferred_element_type=F32).astype(BF)
    keep_ref[...] = result[: HALF // 2]
    send_ref[...] = result[HALF // 2 :]


def project(core, parts, weight):
    width = weight.shape[1]
    tile = 1024
    half = pl.BlockSpec((HALF // 2, tile), lambda n, c: (0, n))
    return pl.pallas_call(
        functools.partial(project_kernel, len(parts)),
        out_shape=[jax.ShapeDtypeStruct((HALF // 2, width), BF)] * 2,
        grid_spec=pltpu.PrefetchScalarGridSpec(
            num_scalar_prefetch=1,
            grid=(width // tile,),
            in_specs=[pl.BlockSpec((HALF, RET_W), lambda n, c: (0, 0))] * len(parts)
            + [pl.BlockSpec((QW, tile), lambda n, c: (0, n))],
            out_specs=[half, half],
            scratch_shapes=[pltpu.VMEM((HALF, QW), BF)],
        ),
        compiler_params=pltpu.CompilerParams(vmem_limit_bytes=56 << 20),
        cost_estimate=pl.CostEstimate(
            flops=4 * HALF * QW * width,
            bytes_accessed=QW * width * 2 + HALF * width * 2,
            transcendentals=0,
        ),
    )(core, *parts, weight)


def after(value, *others):
    return lax.optimization_barrier((value, *others))[0]


def by_halves(value):
    rest = value.shape[1:]
    cut = value.reshape((NEW // (2 * PIECE), 2, PIECE) + rest)
    return jnp.swapaxes(cut, 0, 1).reshape(value.shape)


def per_device(
    queries, new_keys, new_values, positions, cache_keys, cache_values, pattern, out_weight
):
    ctx = lax.axis_index("ctx")
    tp = lax.axis_index("tp")
    core = tp % 2
    x = tp // 2
    y, z = ctx // SIDE, ctx % SIDE

    own_digits = digits(positions)
    q_digits = digits(by_halves(positions))
    q_meta = jnp.concatenate([q_digits.reshape(-1), pattern.reshape(-1).astype(BF)])
    q_meta = jnp.pad(q_meta, (0, META * QW - q_meta.shape[0])).reshape(META, QW)
    k_meta = jnp.pad(own_digits.reshape(-1, HD), ((0, META - 3 * NEW // HD), (0, 0)))
    q_own = jnp.concatenate([by_halves(queries), q_meta], axis=0)
    kv_own = jnp.concatenate([cache_keys, new_keys, cache_values, new_values, k_meta], axis=0)

    q_at = {0: q_own}
    kv_at = {0: kv_own}
    for shift in (1, 3, 2):
        q_at[-shift % SIDE] = move(q_own, "q", shift)

    def segment_at(offset):
        along_y = ((y + offset) % SIDE) * SIDE + z
        along_z = y * SIDE + (z + offset) % SIDE
        return jnp.where(core == 0, along_y, along_z)

    def patterns_at(offset):
        row = q_at[offset][NEW]
        return row[3 * NEW : 3 * NEW + 16].astype(F32).astype(jnp.int32).reshape(4, 4)

    def flags_of(q_offsets, kv_offsets):
        rows = jnp.stack([patterns_at(o) for o in q_offsets])
        segments = jnp.stack([segment_at(o) for o in kv_offsets])
        hits = jnp.any(rows[:, None] == segments[None, :, None, None], axis=-1)
        return hits.astype(jnp.int32).reshape(-1)

    def qpos_of(q_offsets):
        found = [undigits(q_at[o][NEW, : 3 * NEW].reshape(3, NEW)) for o in q_offsets]
        return jnp.broadcast_to(jnp.concatenate(found)[:, None], (NEW * len(found), HD))

    def kpos_of(kv_offsets):
        rows = slice(KV_ROWS - META, KV_ROWS - META + 3 * NEW // HD)
        return jnp.stack([undigits(kv_at[o][rows].reshape(3, NEW))[None] for o in kv_offsets])

    def run(q_offsets, kv_offsets, state=None, final=False, tokens=NEW, part=0):
        return attend(
            flags_of(q_offsets, kv_offsets),
            [q_at[o] for o in q_offsets],
            [kv_at[o] for o in kv_offsets],
            qpos_of(q_offsets),
            kpos_of(kv_offsets),
            state,
            final,
            tokens,
            part,
        )

    away = (1, 3, 2)
    own_state = run((0,), (0,))
    for shift in (1, 3):
        kv_at[-shift % SIDE] = move(after(kv_own, *own_state), "k", shift)
    state = run(away, (0,))
    kv_at[2] = move(after(kv_own, *state), "k", 2)

    def sides(part, start):
        return run(away, (1, 3), start, False, HALF, part)

    def far(part, start):
        return run(away, (2,), start, True, HALF, part)

    def home(part, start):
        return run((0,), (1, 3, 2), start, True, HALF, part)[0]

    def give_back(returns):
        return [move(value, "q", at) for at, value in zip(away, returns)]

    def finish(keep, other):
        def group(shift):
            at = ((x + shift) % XN) * PIECE
            return lax.dynamic_slice_in_dim(keep, at, PIECE, 0).astype(
                F32
            ) + lax.dynamic_slice_in_dim(other, at, PIECE, 0).astype(F32)

        arrived = [move(group(shift).astype(BF), "x", shift) for shift in (1, 3, 2)]
        result = group(0)
        for value in arrived:
            result = result + value.astype(F32)
        return result.astype(BF)

    def chain(start, *others):
        return [after(value, *others) for value in start]

    low = sides(0, state)
    low = far(0, list(low))
    low_back = give_back(low)
    high = sides(1, chain(state, *low))
    low_mine = home(0, chain(own_state, *high))
    keep, send = project(core.reshape(1), [low_mine] + low_back, out_weight)
    other = move(send, "c", 0)
    high = far(1, chain(high, keep))
    high_back = give_back(high)
    first = finish(keep, other)
    high_mine = home(1, chain(own_state, *high))
    keep, send = project(core.reshape(1), [high_mine] + high_back, out_weight)
    second = finish(keep, move(send, "c", 0))
    return jnp.concatenate([first, second], axis=0)


def solution(mesh):
    placed = (
        P("ctx", "tp"),
        P("ctx", "tp"),
        P("ctx", "tp"),
        P("ctx"),
        P("ctx", "tp"),
        P("ctx", "tp"),
        P("ctx", None),
        P("tp", None),
    )

    return jax.shard_map(
        per_device, mesh=mesh, in_specs=placed, out_specs=P(("ctx", "tp"), None), check_vma=False
    )
```

```python
import functools
import math

import jax
import jax.numpy as jnp
from jax import lax
from jax.experimental import pallas as pl
from jax.experimental.pallas import tpu as pltpu
from jax.sharding import PartitionSpec as P


HD = 128
GROUP = 8
SIDE = 4
XN = 4
QB = 64
PIECE = 32
STEP_ROWS = 256
STEP_KEYS = 512
SEG = 2048
NEW = 256
QW = GROUP * HD
META = 16
V_AT = SEG + NEW
RET_W = QW + 128
SEND_W = QW + 128
BASE = 64
NEG = -1e30
SCALE = 1.0 / math.sqrt(HD)
TO_EXP2 = SCALE * math.log2(math.e)
BF = jnp.bfloat16
F32 = jnp.float32
AXES = ("ctx", "tp")


def pairs(kind, shift):
    out = []
    for y in range(SIDE):
        for z in range(SIDE):
            for x in range(XN):
                for c in range(2):
                    to = [y, z, x, c]
                    if kind == "c":
                        to[3] = 1 - c
                    elif kind == "x":
                        to[2] = (x + shift) % XN
                    else:
                        along = (0 if c == 0 else 1) if kind == "k" else (1 if c == 0 else 0)
                        to[along] = (to[along] + shift) % SIDE
                    src = (y * SIDE + z) * 2 * XN + x * 2 + c
                    dst = (to[0] * SIDE + to[1]) * 2 * XN + to[2] * 2 + to[3]
                    out.append((src, dst))
    return out


def move(value, kind, shift):
    return lax.ppermute(value, AXES, pairs(kind, shift))


def digits(positions):
    p = positions.astype(jnp.int32)
    return jnp.stack([p // (BASE * BASE), (p // BASE) % BASE, p % BASE]).astype(BF)


def dot_t(a, b):
    return lax.dot_general(a, b, (((1,), (1,)), ((), ())), preferred_element_type=F32)


def attend_kernel(n_home, n_kv, bases, resume, final, flags, *refs):
    refs = list(refs)
    q_refs = [refs.pop(0) for _ in range(n_home)]
    kv_refs = [refs.pop(0) for _ in range(n_kv)]
    if resume:
        acc_in, ml_in = refs.pop(0), refs.pop(0)
    if final:
        outs = [refs.pop(0) for _ in range(n_home)]
    else:
        acc_out, ml_out = refs.pop(0), refs.pop(0)
    k_scr, v_scr, meta_scr, q_scr, qpos_scr, m_scr, acc_scr, sems = refs
    home_id = pl.program_id(0)
    tokens = NEW
    blocks = NEW // QB

    def fetch(j):
        return (
            pltpu.make_async_copy(kv_refs[j].at[pl.ds(0, V_AT)], k_scr.at[j], sems.at[j, 0]),
            pltpu.make_async_copy(
                kv_refs[j].at[pl.ds(V_AT, V_AT)], v_scr.at[j, :, pl.ds(0, HD)], sems.at[j, 1]
            ),
            pltpu.make_async_copy(
                kv_refs[j].at[pl.ds(2 * V_AT, META)], meta_scr.at[j], sems.at[j, 2]
            ),
        )

    @pl.when(home_id == 0)
    def _():
        for j in range(n_kv):
            for copy in fetch(j):
                copy.start()
        for j in range(n_kv):
            v_scr[j, :, HD:] = jnp.ones((V_AT, HD), BF)

    if n_home == 1:
        q_src = q_refs[0]
    else:
        q_src = q_scr
        for home in range(n_home):

            @pl.when(home_id == home)
            def _(home=home):
                q_scr[...] = q_refs[home][...]

    for h in range(GROUP):
        cols = slice(h * HD, (h + 1) * HD)
        if resume:
            m_scr[:, cols] = jnp.broadcast_to(ml_in[:, h : h + 1], (tokens, HD))
            acc_scr[:, h * 2 * HD : h * 2 * HD + HD] = acc_in[:, cols]
            acc_scr[:, h * 2 * HD + HD : (h + 1) * 2 * HD] = jnp.broadcast_to(
                ml_in[:, GROUP + h : GROUP + h + 1], (tokens, HD)
            )
        else:
            m_scr[:, cols] = jnp.full((tokens, HD), NEG, F32)
            acc_scr[:, h * 2 * HD : (h + 1) * 2 * HD] = jnp.zeros((tokens, 2 * HD), F32)

    @pl.when(home_id == 0)
    def _():
        for j in range(n_kv):
            for copy in fetch(j):
                copy.wait()

    packed = q_src[:, QW:].astype(F32)
    qpos_scr[...] = jnp.broadcast_to(
        packed[:, :1] * (BASE * BASE) + packed[:, 1:2] * BASE + packed[:, 2:3], (tokens, HD)
    )

    def advance(q, m, acc, k, v, mask):
        s = dot_t(q, k)
        if mask is not None:
            s = jnp.where(mask, s, NEG)
        peak = jnp.broadcast_to(jnp.max(s, axis=1, keepdims=True), m.shape)
        top = jnp.maximum(m, peak)
        p = jnp.exp2((s - jnp.concatenate([top] * (s.shape[1] // HD), axis=1)) * TO_EXP2)
        decay = jnp.exp2((m - top) * TO_EXP2)
        acc = acc * jnp.concatenate([decay, decay], axis=1) + jnp.dot(
            p.astype(BF), v, preferred_element_type=F32
        )
        return top, acc

    def fresh(j, carry):
        meta = meta_scr[j].astype(F32)
        parts = [
            jnp.concatenate([meta[2 * n : 2 * n + 1], meta[2 * n + 1 : 2 * n + 2]], axis=1)
            for n in range(3)
        ]
        kpos = parts[0] * (BASE * BASE) + parts[1] * BASE + parts[2]
        qpos = qpos_scr[...]
        mask = kpos <= jnp.concatenate([qpos, qpos], axis=1)
        k = k_scr[j, SEG:, :]
        v = v_scr[j, SEG:, :]
        for h in range(GROUP):
            cols = slice(h * HD, (h + 1) * HD)
            wide = slice(h * 2 * HD, (h + 1) * 2 * HD)
            top, acc = advance(q_src[:, cols], m_scr[:, cols], acc_scr[:, wide], k, v, mask)
            m_scr[:, cols] = top
            acc_scr[:, wide] = acc
        return carry

    per_pass = STEP_ROWS // QB

    def cached(item, carry):
        j, block = item // blocks, item % blocks
        at = ((bases[0] + home_id) * SIDE + bases[1] + j) * blocks + block

        @pl.when(flags[at] > 0)
        def _():
            rows = pl.ds(pl.multiple_of(block * QB, QB), QB)
            for first in range(0, GROUP, per_pass):
                heads = range(first, first + per_pass)
                q = jnp.concatenate([q_src[rows, h * HD : (h + 1) * HD] for h in heads], axis=0)
                m = jnp.concatenate([m_scr[rows, h * HD : (h + 1) * HD] for h in heads], axis=0)
                acc = jnp.concatenate(
                    [acc_scr[rows, h * 2 * HD : (h + 1) * 2 * HD] for h in heads], axis=0
                )
                for n in range(SEG // STEP_KEYS):
                    keys = slice(n * STEP_KEYS, (n + 1) * STEP_KEYS)
                    m, acc = advance(q, m, acc, k_scr[j, keys, :], v_scr[j, keys, :], None)
                for n, h in enumerate(heads):
                    part = slice(n * QB, (n + 1) * QB)
                    m_scr[rows, h * HD : (h + 1) * HD] = m[part]
                    acc_scr[rows, h * 2 * HD : (h + 1) * 2 * HD] = acc[part]

        return carry

    if n_kv == 1:
        fresh(0, 0)
    else:
        lax.fori_loop(0, n_kv, fresh, 0)
    lax.fori_loop(0, n_kv * blocks, cached, 0)

    lane = lax.broadcasted_iota(jnp.int32, (tokens, HD), 1)
    if not final:
        ml = jnp.zeros((tokens, HD), F32)
        for h in range(GROUP):
            acc_out[:, h * HD : (h + 1) * HD] = acc_scr[:, h * 2 * HD : h * 2 * HD + HD]
            ml = jnp.where(lane == h, m_scr[:, h * HD : (h + 1) * HD], ml)
            ml = jnp.where(lane == GROUP + h, acc_scr[:, h * 2 * HD + HD : (h + 1) * 2 * HD], ml)
        ml_out[...] = ml
        return

    def emit(out):
        logs = jnp.zeros((tokens, HD), F32)
        for h in range(GROUP):
            cols = slice(h * HD, (h + 1) * HD)
            total = acc_scr[:, h * 2 * HD + HD : (h + 1) * 2 * HD]
            out[:, cols] = (acc_scr[:, h * 2 * HD : h * 2 * HD + HD] / total).astype(BF)
            log = m_scr[:, cols] * SCALE + jnp.log(total)
            logs = jnp.where(lax.rem(lane, GROUP) == h, log, logs)
        hi = logs.astype(BF).astype(F32)
        mid = (logs - hi).astype(BF).astype(F32)
        parts = jnp.where(lane < GROUP, hi, jnp.where(lane < 2 * GROUP, mid, logs - hi - mid))
        out[:, QW:] = parts.astype(BF)

    for home in range(n_home):
        if n_home == 1:
            emit(outs[0])
        else:
            pl.when(home_id == home)(functools.partial(emit, outs[home]))


def attend(flags, q_list, kv_list, bases, state=None, final=False):
    n_home, n_kv = len(q_list), len(kv_list)
    fixed = lambda shape: pl.BlockSpec(shape, lambda i, f: (0,) * len(shape))
    turn = lambda width: pl.BlockSpec((NEW, width), lambda i, f: (i, 0))
    in_specs = [fixed((NEW, SEND_W))] * n_home + [pl.BlockSpec(memory_space=pl.ANY)] * n_kv
    args = list(q_list) + list(kv_list)
    if state is not None:
        in_specs += [turn(QW), turn(HD)]
        args += list(state)
    if final:
        out_shape = [jax.ShapeDtypeStruct((NEW, RET_W), BF)] * n_home
        out_specs = [fixed((NEW, RET_W))] * n_home
    else:
        out_shape = [
            jax.ShapeDtypeStruct((n_home * NEW, QW), F32),
            jax.ShapeDtypeStruct((n_home * NEW, HD), F32),
        ]
        out_specs = [turn(QW), turn(HD)]
    work = n_home * n_kv * NEW * GROUP * (SEG // 4 + NEW)
    return pl.pallas_call(
        functools.partial(attend_kernel, n_home, n_kv, bases, state is not None, final),
        out_shape=out_shape,
        grid_spec=pltpu.PrefetchScalarGridSpec(
            num_scalar_prefetch=1,
            grid=(n_home,),
            in_specs=in_specs,
            out_specs=out_specs,
            scratch_shapes=[
                pltpu.VMEM((n_kv, V_AT, HD), BF),
                pltpu.VMEM((n_kv, V_AT, 2 * HD), BF),
                pltpu.VMEM((n_kv, META, HD), BF),
                pltpu.VMEM((NEW, SEND_W), BF),
                pltpu.VMEM((NEW, HD), F32),
                pltpu.VMEM((NEW, QW), F32),
                pltpu.VMEM((NEW, 2 * QW), F32),
                pltpu.SemaphoreType.DMA((n_kv, 3)),
            ],
        ),
        compiler_params=pltpu.CompilerParams(vmem_limit_bytes=24 << 20),
        cost_estimate=pl.CostEstimate(
            flops=work * HD * 4 * 2,
            bytes_accessed=n_home * NEW * QW * 8,
            transcendentals=work,
        ),
    )(flags, *args)


def project_kernel(n_parts, core, *refs):
    w_ref, *outs = refs[max(n_parts, 1) :]
    if n_parts == 0:
        att = refs[0]
        keep_ref, send_ref = outs
    else:
        parts = refs[:n_parts]
        keep_ref, send_ref, att = outs

        @pl.when(pl.program_id(0) == 0)
        def _():
            merge(core, parts, att)

    result = jnp.dot(att[...], w_ref[...], preferred_element_type=F32).astype(BF)
    keep_ref[...] = result[: NEW // 2]
    send_ref[...] = result[NEW // 2 :]


def merge(core, parts, att):
    for t in range(NEW // PIECE):
        rows = slice(t * PIECE, (t + 1) * PIECE)
        logs = []
        for part in parts:
            packed = part[rows, QW:].astype(F32)
            logs.append(
                packed[:, :GROUP]
                + packed[:, GROUP : 2 * GROUP]
                + packed[:, 2 * GROUP : 3 * GROUP]
            )
        top = functools.reduce(jnp.maximum, logs)
        shares = [jnp.exp(log - top) for log in logs]
        total = functools.reduce(jnp.add, shares)
        shares = [share / total for share in shares]
        away = jnp.where(core[0] == t % 2, 0, NEW // 2)
        at = pl.multiple_of(away + (t // 2) * PIECE, PIECE)
        for h in range(GROUP):
            mixed = functools.reduce(
                jnp.add,
                [
                    share[:, h : h + 1] * part[rows, h * HD : (h + 1) * HD].astype(F32)
                    for share, part in zip(shares, parts)
                ],
            )
            att[pl.ds(at, PIECE), h * HD : (h + 1) * HD] = mixed.astype(BF)


def project(core, parts, weight, column, columns):
    width = weight.shape[1] // columns
    tile = 1024
    steps = width // tile
    merged = len(parts) == 1
    half = pl.BlockSpec((NEW // 2, tile), lambda n, c: (0, n))
    att_spec = pl.BlockSpec((NEW, QW), lambda n, c: (0, 0))
    out_shape = [jax.ShapeDtypeStruct((NEW // 2, width), BF)] * 2
    out_specs = [half, half]
    if not merged:
        out_shape.append(jax.ShapeDtypeStruct((NEW, QW), BF))
        out_specs.append(att_spec)
    return pl.pallas_call(
        functools.partial(project_kernel, 0 if merged else len(parts)),
        out_shape=out_shape,
        grid_spec=pltpu.PrefetchScalarGridSpec(
            num_scalar_prefetch=1,
            grid=(steps,),
            in_specs=[pl.BlockSpec(part.shape, lambda n, c: (0, 0)) for part in parts]
            + [pl.BlockSpec((QW, tile), lambda n, c: (0, column * steps + n))],
            out_specs=out_specs,
        ),
        compiler_params=pltpu.CompilerParams(vmem_limit_bytes=24 << 20),
        cost_estimate=pl.CostEstimate(
            flops=4 * NEW * QW * width,
            bytes_accessed=QW * width * 2 + NEW * width * 2,
            transcendentals=0,
        ),
    )(core, *parts, weight)


def after(value, *others):
    return lax.optimization_barrier((value, *others))[0]


def per_device(
    queries, new_keys, new_values, positions, cache_keys, cache_values, pattern, out_weight
):
    ctx = lax.axis_index("ctx")
    tp = lax.axis_index("tp")
    core = tp % 2
    x = tp // 2
    y, z = ctx // SIDE, ctx % SIDE

    places = digits(positions)
    picks = pattern.reshape(-1).astype(BF)
    q_own = jnp.concatenate([queries, jnp.pad(places.T, ((0, 0), (0, HD - 3)))], axis=1)
    q_meta = jnp.pad(picks, (0, META * SEND_W - picks.shape[0])).reshape(META, SEND_W)
    q_own = jnp.concatenate([q_own, q_meta], axis=0)
    k_meta = jnp.pad(places.reshape(-1, HD), ((0, META - 3 * NEW // HD), (0, 0)))
    kv_own = jnp.concatenate([cache_keys, new_keys, cache_values, new_values, k_meta], axis=0)

    order = (0, 1, 3, 2)
    q_at = {0: q_own}
    kv_at = {0: kv_own}
    for shift in (1, 3, 2):
        q_at[-shift % SIDE] = move(q_own, "q", shift)

    steps = jnp.array(order, jnp.int32)
    along_y = ((y + steps) % SIDE) * SIDE + z
    along_z = y * SIDE + (z + steps) % SIDE
    segments = jnp.where(core == 0, along_y, along_z).astype(F32)

    def flags_of(rows):
        named = rows.astype(F32).reshape(-1, 1, NEW // QB, picks.shape[0] * QB // NEW)
        hits = jnp.any(named == segments[None, :, None, None], axis=-1)
        return hits.astype(jnp.int32).reshape(-1)

    def state_of(flags, homes, kvs, state=None, final=False):
        return attend(
            flags,
            [q_at[order[n]] for n in homes],
            [kv_at[order[n]] for n in kvs],
            (homes[0], kvs[0]),
            state,
            final,
        )

    away, others = (1, 2, 3), (1, 2, 3)
    own_state = state_of(flags_of(picks[None]), (0,), (0,))
    for shift in (1, 3):
        kv_at[-shift % SIDE] = move(after(kv_own, *own_state), "k", shift)
    flags = flags_of(jnp.stack([q_at[o][NEW, : picks.shape[0]] for o in order]))
    state = state_of(flags, away, (0,))
    kv_at[2] = move(after(kv_own, *state), "k", 2)
    state = state_of(flags, away, (1, 2), state)
    partials = state_of(flags, away, (3,), state, True)
    backs = [move(part, "q", order[n]) for n, part in zip(away, partials)]
    own_state = [after(value, *partials) for value in own_state]
    mine = state_of(flags, (0,), others, own_state, True)

    core_id = core.reshape(1)
    keep0, send0, att = project(core_id, [*mine, *backs], out_weight, 0, 2)
    other0 = move(send0, "c", 0)
    keep1, send1 = project(core_id, [att], out_weight, 1, 2)
    other1 = move(send1, "c", 0)

    def finish(keep, other):
        def group(shift):
            at = ((x + shift) % XN) * PIECE
            return lax.dynamic_slice_in_dim(keep, at, PIECE, 0).astype(
                F32
            ) + lax.dynamic_slice_in_dim(other, at, PIECE, 0).astype(F32)

        arrived = [move(group(shift).astype(BF), "x", shift) for shift in (1, 3, 2)]
        result = group(0)
        for value in arrived:
            result = result + value.astype(F32)
        return result.astype(BF)

    return jnp.concatenate([finish(keep0, other0), finish(keep1, other1)], axis=1)


def solution(mesh):
    placed = (
        P("ctx", "tp"),
        P("ctx", "tp"),
        P("ctx", "tp"),
        P("ctx"),
        P("ctx", "tp"),
        P("ctx", "tp"),
        P("ctx", None),
        P("tp", None),
    )

    return jax.shard_map(
        per_device, mesh=mesh, in_specs=placed, out_specs=P(("ctx", "tp"), None), check_vma=False
    )
```

```python
import functools
import math

import jax
import jax.numpy as jnp
from jax import lax
from jax.experimental import pallas as pl
from jax.experimental.pallas import tpu as pltpu
from jax.sharding import PartitionSpec as P


HD = 128
GROUP = 8
SIDE = 4
XN = 4
QB = 64
PIECE = 32
STEP_ROWS = 256
STEP_KEYS = 512
SEG = 2048
NEW = 256
QW = GROUP * HD
META = 16
V_AT = SEG + NEW
RET_W = QW + 128
SEND_W = QW + 128
BASE = 64
NEG = -1e30
SCALE = 1.0 / math.sqrt(HD)
TO_EXP2 = SCALE * math.log2(math.e)
BF = jnp.bfloat16
F32 = jnp.float32
AXES = ("ctx", "tp")


def pairs(kind, shift):
    out = []
    for y in range(SIDE):
        for z in range(SIDE):
            for x in range(XN):
                for c in range(2):
                    to = [y, z, x, c]
                    if kind == "c":
                        to[3] = 1 - c
                    elif kind == "x":
                        to[2] = (x + shift) % XN
                    else:
                        along = (0 if c == 0 else 1) if kind == "k" else (1 if c == 0 else 0)
                        to[along] = (to[along] + shift) % SIDE
                    src = (y * SIDE + z) * 2 * XN + x * 2 + c
                    dst = (to[0] * SIDE + to[1]) * 2 * XN + to[2] * 2 + to[3]
                    out.append((src, dst))
    return out


def move(value, kind, shift):
    return lax.ppermute(value, AXES, pairs(kind, shift))


def digits(positions):
    p = positions.astype(jnp.int32)
    return jnp.stack([p // (BASE * BASE), (p // BASE) % BASE, p % BASE]).astype(BF)


def dot_t(a, b):
    return lax.dot_general(a, b, (((1,), (1,)), ((), ())), preferred_element_type=F32)


def attend_kernel(n_home, n_kv, first_kv, resume, final, *refs):
    refs = list(refs)
    flags = [refs.pop(0) for _ in range(n_home)]
    q_refs = [refs.pop(0) for _ in range(n_home)]
    kv_refs = [refs.pop(0) for _ in range(n_kv)]
    if resume:
        acc_in, ml_in = refs.pop(0), refs.pop(0)
    if final:
        outs = [refs.pop(0) for _ in range(n_home)]
    else:
        acc_out, ml_out = refs[-10:-8]
    k_scr, v_scr, meta_scr, q_scr, qpos_scr, m_scr, acc_scr, sems = refs[-8:]
    home_id = pl.program_id(0)
    tokens = NEW
    blocks = NEW // QB

    def fetch(j):
        return (
            pltpu.make_async_copy(kv_refs[j].at[pl.ds(0, V_AT)], k_scr.at[j], sems.at[j, 0]),
            pltpu.make_async_copy(
                kv_refs[j].at[pl.ds(V_AT, V_AT)], v_scr.at[j, :, pl.ds(0, HD)], sems.at[j, 1]
            ),
            pltpu.make_async_copy(
                kv_refs[j].at[pl.ds(2 * V_AT, META)], meta_scr.at[j], sems.at[j, 2]
            ),
        )

    @pl.when(home_id == 0)
    def _():
        for j in range(n_kv):
            for copy in fetch(j):
                copy.start()
        for j in range(n_kv):
            v_scr[j, :, HD:] = jnp.ones((V_AT, HD), BF)

    if n_home == 1:
        q_src = q_refs[0]
    else:
        q_src = q_scr
        for home in range(n_home):

            @pl.when(home_id == home)
            def _(home=home):
                q_scr[...] = q_refs[home][...]

    for h in range(GROUP):
        cols = slice(h * HD, (h + 1) * HD)
        if resume:
            m_scr[:, cols] = jnp.broadcast_to(ml_in[:, h : h + 1], (tokens, HD))
            acc_scr[:, h * 2 * HD : h * 2 * HD + HD] = acc_in[:, cols]
            acc_scr[:, h * 2 * HD + HD : (h + 1) * 2 * HD] = jnp.broadcast_to(
                ml_in[:, GROUP + h : GROUP + h + 1], (tokens, HD)
            )
        else:
            m_scr[:, cols] = jnp.full((tokens, HD), NEG, F32)
            acc_scr[:, h * 2 * HD : (h + 1) * 2 * HD] = jnp.zeros((tokens, 2 * HD), F32)

    @pl.when(home_id == 0)
    def _():
        for j in range(n_kv):
            for copy in fetch(j):
                copy.wait()

    packed = q_src[:, QW:].astype(F32)
    qpos_scr[...] = jnp.broadcast_to(
        packed[:, :1] * (BASE * BASE) + packed[:, 1:2] * BASE + packed[:, 2:3], (tokens, HD)
    )

    def advance(q, m, acc, k, v, mask):
        s = dot_t(q, k)
        if mask is not None:
            s = jnp.where(mask, s, NEG)
        peak = jnp.broadcast_to(jnp.max(s, axis=1, keepdims=True), m.shape)
        top = jnp.maximum(m, peak)
        p = jnp.exp2((s - jnp.concatenate([top] * (s.shape[1] // HD), axis=1)) * TO_EXP2)
        decay = jnp.exp2((m - top) * TO_EXP2)
        acc = acc * jnp.concatenate([decay, decay], axis=1) + jnp.dot(
            p.astype(BF), v, preferred_element_type=F32
        )
        return top, acc

    def fresh(j, carry):
        meta = meta_scr[j].astype(F32)
        parts = [
            jnp.concatenate([meta[2 * n : 2 * n + 1], meta[2 * n + 1 : 2 * n + 2]], axis=1)
            for n in range(3)
        ]
        kpos = parts[0] * (BASE * BASE) + parts[1] * BASE + parts[2]
        qpos = qpos_scr[...]
        mask = kpos <= jnp.concatenate([qpos, qpos], axis=1)
        k = k_scr[j, SEG:, :]
        v = v_scr[j, SEG:, :]
        for h in range(GROUP):
            cols = slice(h * HD, (h + 1) * HD)
            wide = slice(h * 2 * HD, (h + 1) * 2 * HD)
            top, acc = advance(q_src[:, cols], m_scr[:, cols], acc_scr[:, wide], k, v, mask)
            m_scr[:, cols] = top
            acc_scr[:, wide] = acc
        return carry

    per_pass = STEP_ROWS // QB

    def cached(item, carry):
        j, block = item // blocks, item % blocks
        at = (first_kv + j) * blocks + block
        hit = flags[0][at]
        for home in range(1, n_home):
            hit = jnp.where(home_id == home, flags[home][at], hit)

        @pl.when(hit > 0)
        def _():
            rows = pl.ds(pl.multiple_of(block * QB, QB), QB)
            for first in range(0, GROUP, per_pass):
                heads = range(first, first + per_pass)
                q = jnp.concatenate([q_src[rows, h * HD : (h + 1) * HD] for h in heads], axis=0)
                m = jnp.concatenate([m_scr[rows, h * HD : (h + 1) * HD] for h in heads], axis=0)
                acc = jnp.concatenate(
                    [acc_scr[rows, h * 2 * HD : (h + 1) * 2 * HD] for h in heads], axis=0
                )
                for n in range(SEG // STEP_KEYS):
                    keys = slice(n * STEP_KEYS, (n + 1) * STEP_KEYS)
                    m, acc = advance(q, m, acc, k_scr[j, keys, :], v_scr[j, keys, :], None)
                for n, h in enumerate(heads):
                    part = slice(n * QB, (n + 1) * QB)
                    m_scr[rows, h * HD : (h + 1) * HD] = m[part]
                    acc_scr[rows, h * 2 * HD : (h + 1) * 2 * HD] = acc[part]

        return carry

    if n_kv == 1:
        fresh(0, 0)
    else:
        lax.fori_loop(0, n_kv, fresh, 0)
    lax.fori_loop(0, n_kv * blocks, cached, 0)

    lane = lax.broadcasted_iota(jnp.int32, (tokens, HD), 1)
    if not final:
        ml = jnp.zeros((tokens, HD), F32)
        for h in range(GROUP):
            acc_out[:, h * HD : (h + 1) * HD] = acc_scr[:, h * 2 * HD : h * 2 * HD + HD]
            ml = jnp.where(lane == h, m_scr[:, h * HD : (h + 1) * HD], ml)
            ml = jnp.where(lane == GROUP + h, acc_scr[:, h * 2 * HD + HD : (h + 1) * 2 * HD], ml)
        ml_out[...] = ml
        return

    def emit(out):
        logs = jnp.zeros((tokens, HD), F32)
        for h in range(GROUP):
            cols = slice(h * HD, (h + 1) * HD)
            total = acc_scr[:, h * 2 * HD + HD : (h + 1) * 2 * HD]
            out[:, cols] = (acc_scr[:, h * 2 * HD : h * 2 * HD + HD] / total).astype(BF)
            log = m_scr[:, cols] * SCALE + jnp.log(total)
            logs = jnp.where(lax.rem(lane, GROUP) == h, log, logs)
        hi = logs.astype(BF).astype(F32)
        mid = (logs - hi).astype(BF).astype(F32)
        parts = jnp.where(lane < GROUP, hi, jnp.where(lane < 2 * GROUP, mid, logs - hi - mid))
        out[:, QW:] = parts.astype(BF)

    for home in range(n_home):
        if n_home == 1:
            emit(outs[0])
        else:
            pl.when(home_id == home)(functools.partial(emit, outs[home]))


def attend(flags, q_list, kv_list, first_kv, state=None, final=False, into=None):
    n_home, n_kv = len(q_list), len(kv_list)
    fixed = lambda shape: pl.BlockSpec(shape, lambda i, *f: (0,) * len(shape))
    turn = lambda width, at=0: pl.BlockSpec((NEW, width), lambda i, *f: (i + at, 0))
    anywhere = pl.BlockSpec(memory_space=pl.ANY)
    in_specs = [fixed((NEW, SEND_W))] * n_home + [anywhere] * n_kv
    args = list(q_list) + list(kv_list)
    aliases = {}
    if state is not None:
        in_specs += [turn(QW), turn(HD)]
        args += list(state)
    if final:
        out_shape = [jax.ShapeDtypeStruct((NEW, RET_W), BF)] * n_home
        out_specs = [fixed((NEW, RET_W))] * n_home
    else:
        places, at, target = into or (n_home, 0, None)
        out_shape = [
            jax.ShapeDtypeStruct((places * NEW, QW), F32),
            jax.ShapeDtypeStruct((places * NEW, HD), F32),
        ]
        out_specs = [turn(QW, at), turn(HD, at)]
        if target is not None:
            aliases = {n_home + len(args): 0, n_home + len(args) + 1: 1}
            in_specs += [anywhere, anywhere]
            args += list(target)
    work = n_home * n_kv * NEW * GROUP * (SEG // 4 + NEW)
    return pl.pallas_call(
        functools.partial(attend_kernel, n_home, n_kv, first_kv, state is not None, final),
        out_shape=out_shape,
        grid_spec=pltpu.PrefetchScalarGridSpec(
            num_scalar_prefetch=n_home,
            grid=(n_home,),
            in_specs=in_specs,
            out_specs=out_specs,
            scratch_shapes=[
                pltpu.VMEM((n_kv, V_AT, HD), BF),
                pltpu.VMEM((n_kv, V_AT, 2 * HD), BF),
                pltpu.VMEM((n_kv, META, HD), BF),
                pltpu.VMEM((NEW, SEND_W), BF),
                pltpu.VMEM((NEW, HD), F32),
                pltpu.VMEM((NEW, QW), F32),
                pltpu.VMEM((NEW, 2 * QW), F32),
                pltpu.SemaphoreType.DMA((n_kv, 3)),
            ],
        ),
        input_output_aliases=aliases,
        compiler_params=pltpu.CompilerParams(vmem_limit_bytes=24 << 20),
        cost_estimate=pl.CostEstimate(
            flops=work * HD * 4 * 2,
            bytes_accessed=n_home * NEW * QW * 8,
            transcendentals=work,
        ),
    )(*flags, *args)


def project_kernel(n_parts, core, *refs):
    w_ref, *outs = refs[max(n_parts, 1) :]
    if n_parts == 0:
        att = refs[0]
        keep_ref, send_ref = outs
    else:
        parts = refs[:n_parts]
        keep_ref, send_ref, att = outs

        @pl.when(pl.program_id(0) == 0)
        def _():
            merge(core, parts, att)

    result = jnp.dot(att[...], w_ref[...], preferred_element_type=F32).astype(BF)
    keep_ref[...] = result[: NEW // 2]
    send_ref[...] = result[NEW // 2 :]


def merge(core, parts, att):
    logs = []
    for part in parts:
        packed = part[:, QW:].astype(F32)
        logs.append(
            packed
            + pltpu.roll(packed, HD - GROUP, axis=1)
            + pltpu.roll(packed, HD - 2 * GROUP, axis=1)
        )
    top = functools.reduce(jnp.maximum, logs)
    shares = [jnp.exp(log - top) for log in logs]
    inverse = 1.0 / functools.reduce(jnp.add, shares)
    shares = [share * inverse for share in shares]
    for h in range(GROUP):
        cols = slice(h * HD, (h + 1) * HD)
        mixed = functools.reduce(
            jnp.add,
            [
                share[:, h : h + 1] * part[:, cols].astype(F32)
                for share, part in zip(shares, parts)
            ],
        ).astype(BF)
        for t in range(NEW // PIECE):
            away = jnp.where(core[0] == t % 2, 0, NEW // 2)
            at = pl.multiple_of(away + (t // 2) * PIECE, PIECE)
            att[pl.ds(at, PIECE), cols] = mixed[t * PIECE : (t + 1) * PIECE]


def project(core, parts, weight, column, columns):
    width = weight.shape[1] // columns
    tile = 1024
    steps = width // tile
    merged = len(parts) == 1
    half = pl.BlockSpec((NEW // 2, tile), lambda n, c: (0, n))
    att_spec = pl.BlockSpec((NEW, QW), lambda n, c: (0, 0))
    out_shape = [jax.ShapeDtypeStruct((NEW // 2, width), BF)] * 2
    out_specs = [half, half]
    if not merged:
        out_shape.append(jax.ShapeDtypeStruct((NEW, QW), BF))
        out_specs.append(att_spec)
    return pl.pallas_call(
        functools.partial(project_kernel, 0 if merged else len(parts)),
        out_shape=out_shape,
        grid_spec=pltpu.PrefetchScalarGridSpec(
            num_scalar_prefetch=1,
            grid=(steps,),
            in_specs=[pl.BlockSpec(part.shape, lambda n, c: (0, 0)) for part in parts]
            + [pl.BlockSpec((QW, tile), lambda n, c: (0, column * steps + n))],
            out_specs=out_specs,
        ),
        compiler_params=pltpu.CompilerParams(vmem_limit_bytes=24 << 20),
        cost_estimate=pl.CostEstimate(
            flops=4 * NEW * QW * width,
            bytes_accessed=QW * width * 2 + NEW * width * 2,
            transcendentals=0,
        ),
    )(core, *parts, weight)


def after(value, *others):
    return lax.optimization_barrier((value, *others))[0]


def per_device(
    queries, new_keys, new_values, positions, cache_keys, cache_values, pattern, out_weight
):
    ctx = lax.axis_index("ctx")
    tp = lax.axis_index("tp")
    core = tp % 2
    x = tp // 2
    y, z = ctx // SIDE, ctx % SIDE

    places = digits(positions)
    picks = pattern.reshape(-1).astype(BF)
    q_own = jnp.concatenate([queries, jnp.pad(places.T, ((0, 0), (0, HD - 3)))], axis=1)
    q_meta = jnp.pad(picks, (0, META * SEND_W - picks.shape[0])).reshape(META, SEND_W)
    q_own = jnp.concatenate([q_own, q_meta], axis=0)
    k_meta = jnp.pad(places.reshape(-1, HD), ((0, META - 3 * NEW // HD), (0, 0)))
    kv_own = jnp.concatenate([cache_keys, new_keys, cache_values, new_values, k_meta], axis=0)

    order = (0, 1, 3, 2)
    q_at = {0: q_own}
    kv_at = {0: kv_own}
    for shift in (1, 3, 2):
        q_at[-shift % SIDE] = move(q_own, "q", shift)

    steps = jnp.array(order, jnp.int32)
    along_y = ((y + steps) % SIDE) * SIDE + z
    along_z = y * SIDE + (z + steps) % SIDE
    segments = jnp.where(core == 0, along_y, along_z).astype(F32)

    def flags_of(row):
        named = row.astype(F32).reshape(1, NEW // QB, -1)
        hits = named == segments[:, None, None]
        return jnp.sum(hits.astype(jnp.int32), axis=-1).reshape(-1)

    flags = {0: flags_of(picks)}

    def read_flags(offsets, done):
        for o in offsets:
            flags[o] = flags_of(after(q_at[o][NEW, : picks.shape[0]], *done))

    def run(homes, kvs, state=None, final=False, into=None):
        offsets = [order[n] for n in homes]
        return attend(
            [flags[o] for o in offsets],
            [q_at[o] for o in offsets],
            [kv_at[order[n]] for n in kvs],
            kvs[0],
            state,
            final,
            into,
        )

    own_state = run((0,), (0,))
    for shift in (1, 3):
        kv_at[-shift % SIDE] = move(after(kv_own, *own_state), "k", shift)
    read_flags((1, 3), own_state)
    state = run((1, 2), (0,), into=(3, 0, None))
    read_flags((2,), state)
    state = run((3,), (0,), into=(3, 2, state))
    kv_at[2] = move(after(kv_own, *state), "k", 2)
    state = run((1, 2, 3), (1, 2), state)
    partials = run((1, 2, 3), (3,), state, True)
    backs = [move(part, "q", order[n]) for n, part in zip((1, 2, 3), partials)]
    own_state = [after(value, *partials) for value in own_state]
    mine = run((0,), (1, 2, 3), own_state, True)

    core_id = core.reshape(1)
    keep0, send0, att = project(core_id, [*mine, *backs], out_weight, 0, 2)
    other0 = move(send0, "c", 0)
    keep1, send1 = project(core_id, [att], out_weight, 1, 2)
    other1 = move(send1, "c", 0)

    def finish(keep, other, way):
        def group(shift):
            at = ((x + shift) % XN) * PIECE
            return lax.dynamic_slice_in_dim(keep, at, PIECE, 0).astype(
                F32
            ) + lax.dynamic_slice_in_dim(other, at, PIECE, 0).astype(F32)

        back = -way % XN
        relay = move(group(2).astype(BF), "x", way)
        direct = move(group(back).astype(BF), "x", back)
        joined = (group(way) + relay.astype(F32)).astype(BF)
        joint = move(joined, "x", way)
        return (group(0) + direct.astype(F32) + joint.astype(F32)).astype(BF)

    return jnp.concatenate([finish(keep0, other0, 1), finish(keep1, other1, 3)], axis=1)


def solution(mesh):
    placed = (
        P("ctx", "tp"),
        P("ctx", "tp"),
        P("ctx", "tp"),
        P("ctx"),
        P("ctx", "tp"),
        P("ctx", "tp"),
        P("ctx", None),
        P("tp", None),
    )

    return jax.shard_map(
        per_device, mesh=mesh, in_specs=placed, out_specs=P(("ctx", "tp"), None), check_vma=False
    )
```

```python
import functools
import math

import jax
import jax.numpy as jnp
from jax import lax
from jax.experimental import pallas as pl
from jax.experimental.pallas import tpu as pltpu
from jax.sharding import PartitionSpec as P


HD = 128
GROUP = 8
SIDE = 4
XN = 4
QB = 64
PIECE = 32
STEP_ROWS = 256
STEP_KEYS = 512
SEG = 2048
NEW = 256
QW = GROUP * HD
META = 16
V_AT = SEG + NEW
RET_W = QW + 128
SEND_W = QW + 128
BASE = 64
NEG = -1e30
SCALE = 1.0 / math.sqrt(HD)
TO_EXP2 = SCALE * math.log2(math.e)
BF = jnp.bfloat16
F32 = jnp.float32
AXES = ("ctx", "tp")


def pairs(kind, shift):
    out = []
    for y in range(SIDE):
        for z in range(SIDE):
            for x in range(XN):
                for c in range(2):
                    to = [y, z, x, c]
                    if kind == "c":
                        to[3] = 1 - c
                    elif kind == "x":
                        to[2] = (x + shift) % XN
                    else:
                        along = (0 if c == 0 else 1) if kind == "k" else (1 if c == 0 else 0)
                        to[along] = (to[along] + shift) % SIDE
                    src = (y * SIDE + z) * 2 * XN + x * 2 + c
                    dst = (to[0] * SIDE + to[1]) * 2 * XN + to[2] * 2 + to[3]
                    out.append((src, dst))
    return out


def move(value, kind, shift):
    return lax.ppermute(value, AXES, pairs(kind, shift))


def digits(positions):
    p = positions.astype(jnp.int32)
    return jnp.stack([p // (BASE * BASE), (p // BASE) % BASE, p % BASE]).astype(BF)


def dot_t(a, b):
    return lax.dot_general(a, b, (((1,), (1,)), ((), ())), preferred_element_type=F32)


def attend_kernel(n_home, n_kv, first_kv, resume, final, *refs):
    refs = list(refs)
    flags = [refs.pop(0) for _ in range(n_home)]
    q_refs = [refs.pop(0) for _ in range(n_home)]
    kv_refs = [refs.pop(0) for _ in range(n_kv)]
    if resume:
        acc_in, ml_in = refs.pop(0), refs.pop(0)
    if final:
        outs = [refs.pop(0) for _ in range(n_home)]
    else:
        acc_out, ml_out, token = refs[-11:-8]
    k_scr, v_scr, meta_scr, q_scr, qpos_scr, m_scr, acc_scr, sems = refs[-8:]
    home_id = pl.program_id(0)
    tokens = NEW
    blocks = NEW // QB

    def fetch(j):
        return (
            pltpu.make_async_copy(kv_refs[j].at[pl.ds(0, V_AT)], k_scr.at[j], sems.at[j, 0]),
            pltpu.make_async_copy(
                kv_refs[j].at[pl.ds(V_AT, V_AT)], v_scr.at[j, :, pl.ds(0, HD)], sems.at[j, 1]
            ),
            pltpu.make_async_copy(
                kv_refs[j].at[pl.ds(2 * V_AT, META)], meta_scr.at[j], sems.at[j, 2]
            ),
        )

    @pl.when(home_id == 0)
    def _():
        for j in range(n_kv):
            for copy in fetch(j):
                copy.start()
        for j in range(n_kv):
            v_scr[j, :, HD:] = jnp.ones((V_AT, HD), BF)

    if n_home == 1:
        q_src = q_refs[0]
    else:
        q_src = q_scr
        for home in range(n_home):

            @pl.when(home_id == home)
            def _(home=home):
                q_scr[...] = q_refs[home][...]

    for h in range(GROUP):
        cols = slice(h * HD, (h + 1) * HD)
        if resume:
            m_scr[:, cols] = jnp.broadcast_to(ml_in[:, h : h + 1], (tokens, HD))
            acc_scr[:, h * 2 * HD : h * 2 * HD + HD] = acc_in[:, cols]
            acc_scr[:, h * 2 * HD + HD : (h + 1) * 2 * HD] = jnp.broadcast_to(
                ml_in[:, GROUP + h : GROUP + h + 1], (tokens, HD)
            )
        else:
            m_scr[:, cols] = jnp.full((tokens, HD), NEG, F32)
            acc_scr[:, h * 2 * HD : (h + 1) * 2 * HD] = jnp.zeros((tokens, 2 * HD), F32)

    @pl.when(home_id == 0)
    def _():
        for j in range(n_kv):
            for copy in fetch(j):
                copy.wait()

    packed = q_src[:, QW:].astype(F32)
    qpos_scr[...] = jnp.broadcast_to(
        packed[:, :1] * (BASE * BASE) + packed[:, 1:2] * BASE + packed[:, 2:3], (tokens, HD)
    )

    def advance(q, m, acc, k, v, mask):
        s = dot_t(q, k)
        if mask is not None:
            s = jnp.where(mask, s, NEG)
        peak = jnp.broadcast_to(jnp.max(s, axis=1, keepdims=True), m.shape)
        top = jnp.maximum(m, peak)
        p = jnp.exp2((s - jnp.concatenate([top] * (s.shape[1] // HD), axis=1)) * TO_EXP2)
        decay = jnp.exp2((m - top) * TO_EXP2)
        acc = acc * jnp.concatenate([decay, decay], axis=1) + jnp.dot(
            p.astype(BF), v, preferred_element_type=F32
        )
        return top, acc

    def fresh(j, carry):
        meta = meta_scr[j].astype(F32)
        parts = [
            jnp.concatenate([meta[2 * n : 2 * n + 1], meta[2 * n + 1 : 2 * n + 2]], axis=1)
            for n in range(3)
        ]
        kpos = parts[0] * (BASE * BASE) + parts[1] * BASE + parts[2]
        qpos = qpos_scr[...]
        mask = kpos <= jnp.concatenate([qpos, qpos], axis=1)
        k = k_scr[j, SEG:, :]
        v = v_scr[j, SEG:, :]
        for h in range(GROUP):
            cols = slice(h * HD, (h + 1) * HD)
            wide = slice(h * 2 * HD, (h + 1) * 2 * HD)
            top, acc = advance(q_src[:, cols], m_scr[:, cols], acc_scr[:, wide], k, v, mask)
            m_scr[:, cols] = top
            acc_scr[:, wide] = acc
        return carry

    per_pass = STEP_ROWS // QB

    def cached(item, carry):
        j, block = item // blocks, item % blocks
        at = (first_kv + j) * blocks + block
        hit = flags[0][at]
        for home in range(1, n_home):
            hit = jnp.where(home_id == home, flags[home][at], hit)

        @pl.when(hit > 0)
        def _():
            rows = pl.ds(pl.multiple_of(block * QB, QB), QB)
            for first in range(0, GROUP, per_pass):
                heads = range(first, first + per_pass)
                q = jnp.concatenate([q_src[rows, h * HD : (h + 1) * HD] for h in heads], axis=0)
                m = jnp.concatenate([m_scr[rows, h * HD : (h + 1) * HD] for h in heads], axis=0)
                acc = jnp.concatenate(
                    [acc_scr[rows, h * 2 * HD : (h + 1) * 2 * HD] for h in heads], axis=0
                )
                for n in range(SEG // STEP_KEYS):
                    keys = slice(n * STEP_KEYS, (n + 1) * STEP_KEYS)
                    m, acc = advance(q, m, acc, k_scr[j, keys, :], v_scr[j, keys, :], None)
                for n, h in enumerate(heads):
                    part = slice(n * QB, (n + 1) * QB)
                    m_scr[rows, h * HD : (h + 1) * HD] = m[part]
                    acc_scr[rows, h * 2 * HD : (h + 1) * 2 * HD] = acc[part]

        return carry

    if n_kv == 1:
        fresh(0, 0)
    else:
        lax.fori_loop(0, n_kv, fresh, 0)
    lax.fori_loop(0, n_kv * blocks, cached, 0)

    lane = lax.broadcasted_iota(jnp.int32, (tokens, HD), 1)
    if not final:
        ml = jnp.zeros((tokens, HD), F32)
        for h in range(GROUP):
            acc_out[:, h * HD : (h + 1) * HD] = acc_scr[:, h * 2 * HD : h * 2 * HD + HD]
            ml = jnp.where(lane == h, m_scr[:, h * HD : (h + 1) * HD], ml)
            ml = jnp.where(lane == GROUP + h, acc_scr[:, h * 2 * HD + HD : (h + 1) * 2 * HD], ml)
        ml_out[...] = ml
        token[...] = jnp.zeros(token.shape, F32)
        return

    def emit(out):
        logs = jnp.zeros((tokens, HD), F32)
        for h in range(GROUP):
            cols = slice(h * HD, (h + 1) * HD)
            total = acc_scr[:, h * 2 * HD + HD : (h + 1) * 2 * HD]
            out[:, cols] = (acc_scr[:, h * 2 * HD : h * 2 * HD + HD] / total).astype(BF)
            log = m_scr[:, cols] * SCALE + jnp.log(total)
            logs = jnp.where(lax.rem(lane, GROUP) == h, log, logs)
        hi = logs.astype(BF).astype(F32)
        mid = (logs - hi).astype(BF).astype(F32)
        parts = jnp.where(lane < GROUP, hi, jnp.where(lane < 2 * GROUP, mid, logs - hi - mid))
        out[:, QW:] = parts.astype(BF)

    for home in range(n_home):
        if n_home == 1:
            emit(outs[0])
        else:
            pl.when(home_id == home)(functools.partial(emit, outs[home]))


def attend(flags, q_list, kv_list, first_kv, state=None, final=False, into=None):
    n_home, n_kv = len(q_list), len(kv_list)
    fixed = lambda shape: pl.BlockSpec(shape, lambda i, *f: (0,) * len(shape))
    turn = lambda width, at=0: pl.BlockSpec((NEW, width), lambda i, *f: (i + at, 0))
    anywhere = pl.BlockSpec(memory_space=pl.ANY)
    in_specs = [fixed((NEW, SEND_W))] * n_home + [anywhere] * n_kv
    args = list(q_list) + list(kv_list)
    aliases = {}
    if state is not None:
        in_specs += [turn(QW), turn(HD)]
        args += list(state[:2])
    if final:
        out_shape = [jax.ShapeDtypeStruct((NEW, RET_W), BF)] * n_home
        out_specs = [fixed((NEW, RET_W))] * n_home
    else:
        places, at, target = into or (n_home, 0, None)
        out_shape = [
            jax.ShapeDtypeStruct((places * NEW, QW), F32),
            jax.ShapeDtypeStruct((places * NEW, HD), F32),
            jax.ShapeDtypeStruct((8, HD), F32),
        ]
        out_specs = [turn(QW, at), turn(HD, at), fixed((8, HD))]
        if target is not None:
            aliases = {n_home + len(args): 0, n_home + len(args) + 1: 1}
            in_specs += [anywhere, anywhere]
            args += list(target[:2])
    work = n_home * n_kv * NEW * GROUP * (SEG // 4 + NEW)
    return pl.pallas_call(
        functools.partial(attend_kernel, n_home, n_kv, first_kv, state is not None, final),
        out_shape=out_shape,
        grid_spec=pltpu.PrefetchScalarGridSpec(
            num_scalar_prefetch=n_home,
            grid=(n_home,),
            in_specs=in_specs,
            out_specs=out_specs,
            scratch_shapes=[
                pltpu.VMEM((n_kv, V_AT, HD), BF),
                pltpu.VMEM((n_kv, V_AT, 2 * HD), BF),
                pltpu.VMEM((n_kv, META, HD), BF),
                pltpu.VMEM((NEW, SEND_W), BF),
                pltpu.VMEM((NEW, HD), F32),
                pltpu.VMEM((NEW, QW), F32),
                pltpu.VMEM((NEW, 2 * QW), F32),
                pltpu.SemaphoreType.DMA((n_kv, 3)),
            ],
        ),
        input_output_aliases=aliases,
        compiler_params=pltpu.CompilerParams(vmem_limit_bytes=24 << 20),
        cost_estimate=pl.CostEstimate(
            flops=work * HD * 4 * 2,
            bytes_accessed=n_home * NEW * QW * 8,
            transcendentals=work,
        ),
    )(*flags, *args)


def project_kernel(n_parts, core, *refs):
    w_ref, *outs = refs[max(n_parts, 1) :]
    if n_parts == 0:
        att = refs[0]
        keep_ref, send_ref = outs
    else:
        parts = refs[:n_parts]
        keep_ref, send_ref, att = outs

        @pl.when(pl.program_id(0) == 0)
        def _():
            merge(core, parts, att)

    result = jnp.dot(att[...], w_ref[...], preferred_element_type=F32).astype(BF)
    keep_ref[...] = result[: NEW // 2]
    send_ref[...] = result[NEW // 2 :]


def merge(core, parts, att):
    logs = []
    for part in parts:
        packed = part[:, QW:].astype(F32)
        logs.append(
            packed
            + pltpu.roll(packed, HD - GROUP, axis=1)
            + pltpu.roll(packed, HD - 2 * GROUP, axis=1)
        )
    top = functools.reduce(jnp.maximum, logs)
    shares = [jnp.exp(log - top) for log in logs]
    inverse = 1.0 / functools.reduce(jnp.add, shares)
    shares = [share * inverse for share in shares]
    for h in range(GROUP):
        cols = slice(h * HD, (h + 1) * HD)
        mixed = functools.reduce(
            jnp.add,
            [
                share[:, h : h + 1] * part[:, cols].astype(F32)
                for share, part in zip(shares, parts)
            ],
        ).astype(BF)
        for t in range(NEW // PIECE):
            away = jnp.where(core[0] == t % 2, 0, NEW // 2)
            at = pl.multiple_of(away + (t // 2) * PIECE, PIECE)
            att[pl.ds(at, PIECE), cols] = mixed[t * PIECE : (t + 1) * PIECE]


def project(core, parts, weight, column, columns):
    width = weight.shape[1] // columns
    tile = 1024
    steps = width // tile
    merged = len(parts) == 1
    half = pl.BlockSpec((NEW // 2, tile), lambda n, c: (0, n))
    att_spec = pl.BlockSpec((NEW, QW), lambda n, c: (0, 0))
    out_shape = [jax.ShapeDtypeStruct((NEW // 2, width), BF)] * 2
    out_specs = [half, half]
    if not merged:
        out_shape.append(jax.ShapeDtypeStruct((NEW, QW), BF))
        out_specs.append(att_spec)
    return pl.pallas_call(
        functools.partial(project_kernel, 0 if merged else len(parts)),
        out_shape=out_shape,
        grid_spec=pltpu.PrefetchScalarGridSpec(
            num_scalar_prefetch=1,
            grid=(steps,),
            in_specs=[pl.BlockSpec(part.shape, lambda n, c: (0, 0)) for part in parts]
            + [pl.BlockSpec((QW, tile), lambda n, c: (0, column * steps + n))],
            out_specs=out_specs,
        ),
        compiler_params=pltpu.CompilerParams(vmem_limit_bytes=24 << 20),
        cost_estimate=pl.CostEstimate(
            flops=4 * NEW * QW * width,
            bytes_accessed=QW * width * 2 + NEW * width * 2,
            transcendentals=0,
        ),
    )(core, *parts, weight)


def per_device(
    queries, new_keys, new_values, positions, cache_keys, cache_values, pattern, out_weight
):
    ctx = lax.axis_index("ctx")
    tp = lax.axis_index("tp")
    core = tp % 2
    x = tp // 2
    y, z = ctx // SIDE, ctx % SIDE

    places = digits(positions)
    picks = pattern.reshape(-1).astype(BF)
    q_own = jnp.concatenate([queries, jnp.pad(places.T, ((0, 0), (0, HD - 3)))], axis=1)
    q_meta = jnp.pad(picks, (0, META * SEND_W - picks.shape[0])).reshape(META, SEND_W)
    q_own = jnp.concatenate([q_own, q_meta], axis=0)
    k_meta = jnp.pad(places.reshape(-1, HD), ((0, META - 3 * NEW // HD), (0, 0)))
    kv_own = jnp.concatenate([cache_keys, new_keys, cache_values, new_values, k_meta], axis=0)

    order = (0, 1, 3, 2)
    q_at = {0: q_own}
    kv_at = {0: kv_own}
    for shift in (1, 3, 2):
        q_at[-shift % SIDE] = move(q_own, "q", shift)

    steps = jnp.array(order, jnp.int32)
    along_y = ((y + steps) % SIDE) * SIDE + z
    along_z = y * SIDE + (z + steps) % SIDE
    segments = jnp.where(core == 0, along_y, along_z).astype(F32)

    def flags_of(row, zero=0.0):
        named = (row.astype(F32) + zero).reshape(1, NEW // QB, -1)
        hits = named == segments[:, None, None]
        return jnp.sum(hits.astype(jnp.int32), axis=-1).reshape(-1)

    flags = {0: flags_of(picks)}

    def read_flags(offsets, done):
        for o in offsets:
            flags[o] = flags_of(q_at[o][NEW, : picks.shape[0]], done[0, 0])

    def run(homes, kvs, state=None, final=False, into=None):
        offsets = [order[n] for n in homes]
        return attend(
            [flags[o] for o in offsets],
            [q_at[o] for o in offsets],
            [kv_at[order[n]] for n in kvs],
            kvs[0],
            state,
            final,
            into,
        )

    own_state = run((0,), (0,))
    for shift in (1, 3):
        kv_at[-shift % SIDE] = move(kv_own, "k", shift)
    read_flags((1, 3), own_state[2])
    state = run((1, 2), (0,), into=(3, 0, None))
    read_flags((2,), state[2])
    state = run((3,), (0,), into=(3, 2, state))
    kv_at[2] = move(kv_own, "k", 2)
    state = run((1, 2, 3), (1, 2), state)
    partials = run((1, 2, 3), (3,), state, True)
    backs = [move(part, "q", order[n]) for n, part in zip((1, 2, 3), partials)]
    mine = run((0,), (1, 2, 3), own_state, True)

    core_id = core.reshape(1)
    keep0, send0, att = project(core_id, [*mine, *backs], out_weight, 0, 2)
    other0 = move(send0, "c", 0)
    keep1, send1 = project(core_id, [att], out_weight, 1, 2)
    other1 = move(send1, "c", 0)

    def finish(keep, other, way):
        def group(shift):
            at = ((x + shift) % XN) * PIECE
            return lax.dynamic_slice_in_dim(keep, at, PIECE, 0).astype(
                F32
            ) + lax.dynamic_slice_in_dim(other, at, PIECE, 0).astype(F32)

        back = -way % XN
        relay = move(group(2).astype(BF), "x", way)
        direct = move(group(back).astype(BF), "x", back)
        joined = (group(way) + relay.astype(F32)).astype(BF)
        joint = move(joined, "x", way)
        return (group(0) + direct.astype(F32) + joint.astype(F32)).astype(BF)

    return jnp.concatenate([finish(keep0, other0, 1), finish(keep1, other1, 3)], axis=1)


def solution(mesh):
    placed = (
        P("ctx", "tp"),
        P("ctx", "tp"),
        P("ctx", "tp"),
        P("ctx"),
        P("ctx", "tp"),
        P("ctx", "tp"),
        P("ctx", None),
        P("tp", None),
    )

    return jax.shard_map(
        per_device, mesh=mesh, in_specs=placed, out_specs=P(("ctx", "tp"), None), check_vma=False
    )
```

```python
import functools
import math

import jax
import jax.numpy as jnp
from jax import lax
from jax.experimental import pallas as pl
from jax.experimental.pallas import tpu as pltpu
from jax.sharding import PartitionSpec as P


HD = 128
GROUP = 8
SIDE = 4
XN = 4
QB = 64
PIECE = 32
STEP_ROWS = 256
STEP_KEYS = 512
SEG = 2048
NEW = 256
QW = GROUP * HD
META = 16
V_AT = SEG + NEW
RET_W = QW + 128
SEND_W = QW + 128
BASE = 64
NEG = -1e30
SCALE = 1.0 / math.sqrt(HD)
TO_EXP2 = SCALE * math.log2(math.e)
BF = jnp.bfloat16
F32 = jnp.float32
AXES = ("ctx", "tp")


def pairs(kind, shift):
    out = []
    for y in range(SIDE):
        for z in range(SIDE):
            for x in range(XN):
                for c in range(2):
                    to = [y, z, x, c]
                    if kind == "c":
                        to[3] = 1 - c
                    elif kind == "x":
                        to[2] = (x + shift) % XN
                    else:
                        along = (0 if c == 0 else 1) if kind == "k" else (1 if c == 0 else 0)
                        to[along] = (to[along] + shift) % SIDE
                    src = (y * SIDE + z) * 2 * XN + x * 2 + c
                    dst = (to[0] * SIDE + to[1]) * 2 * XN + to[2] * 2 + to[3]
                    out.append((src, dst))
    return out


def move(value, kind, shift):
    return lax.ppermute(value, AXES, pairs(kind, shift))


def digits(positions):
    p = positions.astype(jnp.int32)
    return jnp.stack([p // (BASE * BASE), (p // BASE) % BASE, p % BASE]).astype(BF)


def dot_t(a, b):
    return lax.dot_general(a, b, (((1,), (1,)), ((), ())), preferred_element_type=F32)


def attend_kernel(n_home, n_kv, first_kv, resume, final, *refs):
    refs = list(refs)
    segments = refs.pop(0)
    named = [refs.pop(0) for _ in range(n_home)]
    q_refs = [refs.pop(0) for _ in range(n_home)]
    kv_refs = [refs.pop(0) for _ in range(n_kv)]
    if resume:
        acc_in, ml_in = refs.pop(0), refs.pop(0)
    if final:
        outs = [refs.pop(0) for _ in range(n_home)]
    else:
        acc_out, ml_out = refs[-10:-8]
    k_scr, v_scr, meta_scr, q_scr, qpos_scr, m_scr, acc_scr, sems = refs[-8:]
    home_id = pl.program_id(0)
    tokens = NEW
    blocks = NEW // QB

    def fetch(j):
        return (
            pltpu.make_async_copy(kv_refs[j].at[pl.ds(0, V_AT)], k_scr.at[j], sems.at[j, 0]),
            pltpu.make_async_copy(
                kv_refs[j].at[pl.ds(V_AT, V_AT)], v_scr.at[j, :, pl.ds(0, HD)], sems.at[j, 1]
            ),
            pltpu.make_async_copy(
                kv_refs[j].at[pl.ds(2 * V_AT, META)], meta_scr.at[j], sems.at[j, 2]
            ),
        )

    @pl.when(home_id == 0)
    def _():
        for j in range(n_kv):
            for copy in fetch(j):
                copy.start()
        for j in range(n_kv):
            v_scr[j, :, HD:] = jnp.ones((V_AT, HD), BF)

    if n_home == 1:
        q_src = q_refs[0]
    else:
        q_src = q_scr
        for home in range(n_home):

            @pl.when(home_id == home)
            def _(home=home):
                q_scr[...] = q_refs[home][...]

    for h in range(GROUP):
        cols = slice(h * HD, (h + 1) * HD)
        if resume:
            m_scr[:, cols] = jnp.broadcast_to(ml_in[:, h : h + 1], (tokens, HD))
            acc_scr[:, h * 2 * HD : h * 2 * HD + HD] = acc_in[:, cols]
            acc_scr[:, h * 2 * HD + HD : (h + 1) * 2 * HD] = jnp.broadcast_to(
                ml_in[:, GROUP + h : GROUP + h + 1], (tokens, HD)
            )
        else:
            m_scr[:, cols] = jnp.full((tokens, HD), NEG, F32)
            acc_scr[:, h * 2 * HD : (h + 1) * 2 * HD] = jnp.zeros((tokens, 2 * HD), F32)

    @pl.when(home_id == 0)
    def _():
        for j in range(n_kv):
            for copy in fetch(j):
                copy.wait()

    packed = q_src[:, QW:].astype(F32)
    qpos_scr[...] = jnp.broadcast_to(
        packed[:, :1] * (BASE * BASE) + packed[:, 1:2] * BASE + packed[:, 2:3], (tokens, HD)
    )

    def advance(q, m, acc, k, v, mask):
        s = dot_t(q, k)
        if mask is not None:
            s = jnp.where(mask, s, NEG)
        peak = jnp.broadcast_to(jnp.max(s, axis=1, keepdims=True), m.shape)
        top = jnp.maximum(m, peak)
        p = jnp.exp2((s - jnp.concatenate([top] * (s.shape[1] // HD), axis=1)) * TO_EXP2)
        decay = jnp.exp2((m - top) * TO_EXP2)
        acc = acc * jnp.concatenate([decay, decay], axis=1) + jnp.dot(
            p.astype(BF), v, preferred_element_type=F32
        )
        return top, acc

    def fresh(j, carry):
        meta = meta_scr[j].astype(F32)
        parts = [
            jnp.concatenate([meta[2 * n : 2 * n + 1], meta[2 * n + 1 : 2 * n + 2]], axis=1)
            for n in range(3)
        ]
        kpos = parts[0] * (BASE * BASE) + parts[1] * BASE + parts[2]
        qpos = qpos_scr[...]
        mask = kpos <= jnp.concatenate([qpos, qpos], axis=1)
        k = k_scr[j, SEG:, :]
        v = v_scr[j, SEG:, :]
        for h in range(GROUP):
            cols = slice(h * HD, (h + 1) * HD)
            wide = slice(h * 2 * HD, (h + 1) * 2 * HD)
            top, acc = advance(q_src[:, cols], m_scr[:, cols], acc_scr[:, wide], k, v, mask)
            m_scr[:, cols] = top
            acc_scr[:, wide] = acc
        return carry

    per_pass = STEP_ROWS // QB
    picks = SIDE

    def cached(item, carry):
        j, block = item // blocks, item % blocks
        segment = segments[first_kv + j]
        hit = False
        for home in range(n_home):
            for pick in range(picks):
                same = named[home][block * picks + pick] == segment
                hit = jnp.logical_or(hit, jnp.logical_and(home_id == home, same))

        @pl.when(hit)
        def _():
            rows = pl.ds(pl.multiple_of(block * QB, QB), QB)
            for first in range(0, GROUP, per_pass):
                heads = range(first, first + per_pass)
                q = jnp.concatenate([q_src[rows, h * HD : (h + 1) * HD] for h in heads], axis=0)
                m = jnp.concatenate([m_scr[rows, h * HD : (h + 1) * HD] for h in heads], axis=0)
                acc = jnp.concatenate(
                    [acc_scr[rows, h * 2 * HD : (h + 1) * 2 * HD] for h in heads], axis=0
                )
                for n in range(SEG // STEP_KEYS):
                    keys = slice(n * STEP_KEYS, (n + 1) * STEP_KEYS)
                    m, acc = advance(q, m, acc, k_scr[j, keys, :], v_scr[j, keys, :], None)
                for n, h in enumerate(heads):
                    part = slice(n * QB, (n + 1) * QB)
                    m_scr[rows, h * HD : (h + 1) * HD] = m[part]
                    acc_scr[rows, h * 2 * HD : (h + 1) * 2 * HD] = acc[part]

        return carry

    if n_kv == 1:
        fresh(0, 0)
    else:
        lax.fori_loop(0, n_kv, fresh, 0)
    lax.fori_loop(0, n_kv * blocks, cached, 0)

    lane = lax.broadcasted_iota(jnp.int32, (tokens, HD), 1)
    if not final:
        ml = jnp.zeros((tokens, HD), F32)
        for h in range(GROUP):
            acc_out[:, h * HD : (h + 1) * HD] = acc_scr[:, h * 2 * HD : h * 2 * HD + HD]
            ml = jnp.where(lane == h, m_scr[:, h * HD : (h + 1) * HD], ml)
            ml = jnp.where(lane == GROUP + h, acc_scr[:, h * 2 * HD + HD : (h + 1) * 2 * HD], ml)
        ml_out[...] = ml
        return

    def emit(out):
        logs = jnp.zeros((tokens, HD), F32)
        for h in range(GROUP):
            cols = slice(h * HD, (h + 1) * HD)
            total = acc_scr[:, h * 2 * HD + HD : (h + 1) * 2 * HD]
            out[:, cols] = (acc_scr[:, h * 2 * HD : h * 2 * HD + HD] / total).astype(BF)
            log = m_scr[:, cols] * SCALE + jnp.log(total)
            logs = jnp.where(lax.rem(lane, GROUP) == h, log, logs)
        hi = logs.astype(BF).astype(F32)
        mid = (logs - hi).astype(BF).astype(F32)
        parts = jnp.where(lane < GROUP, hi, jnp.where(lane < 2 * GROUP, mid, logs - hi - mid))
        out[:, QW:] = parts.astype(BF)

    for home in range(n_home):
        if n_home == 1:
            emit(outs[0])
        else:
            pl.when(home_id == home)(functools.partial(emit, outs[home]))


def attend(segments, named, q_list, kv_list, first_kv, state=None, final=False, into=None, room=61):
    n_home, n_kv = len(q_list), len(kv_list)
    fixed = lambda shape: pl.BlockSpec(shape, lambda i, *f: (0,) * len(shape))
    turn = lambda width, at=0: pl.BlockSpec((NEW, width), lambda i, *f: (i + at, 0))
    anywhere = pl.BlockSpec(memory_space=pl.ANY)
    in_specs = [fixed((NEW, SEND_W))] * n_home + [anywhere] * n_kv
    args = list(q_list) + list(kv_list)
    aliases = {}
    if state is not None:
        in_specs += [turn(QW), turn(HD)]
        args += list(state)
    if final:
        out_shape = [jax.ShapeDtypeStruct((NEW, RET_W), BF)] * n_home
        out_specs = [fixed((NEW, RET_W))] * n_home
    else:
        places, at, target = into or (n_home, 0, None)
        out_shape = [
            jax.ShapeDtypeStruct((places * NEW, QW), F32),
            jax.ShapeDtypeStruct((places * NEW, HD), F32),
        ]
        out_specs = [turn(QW, at), turn(HD, at)]
        if target is not None:
            aliases = {n_home + 1 + len(args): 0, n_home + 2 + len(args): 1}
            in_specs += [anywhere, anywhere]
            args += list(target)
    work = n_home * n_kv * NEW * GROUP * (SEG // 4 + NEW)
    return pl.pallas_call(
        functools.partial(attend_kernel, n_home, n_kv, first_kv, state is not None, final),
        out_shape=out_shape,
        grid_spec=pltpu.PrefetchScalarGridSpec(
            num_scalar_prefetch=n_home + 1,
            grid=(n_home,),
            in_specs=in_specs,
            out_specs=out_specs,
            scratch_shapes=[
                pltpu.VMEM((n_kv, V_AT, HD), BF),
                pltpu.VMEM((n_kv, V_AT, 2 * HD), BF),
                pltpu.VMEM((n_kv, META, HD), BF),
                pltpu.VMEM((NEW, SEND_W), BF),
                pltpu.VMEM((NEW, HD), F32),
                pltpu.VMEM((NEW, QW), F32),
                pltpu.VMEM((NEW, 2 * QW), F32),
                pltpu.SemaphoreType.DMA((n_kv, 3)),
            ],
        ),
        input_output_aliases=aliases,
        compiler_params=pltpu.CompilerParams(vmem_limit_bytes=room << 20),
        cost_estimate=pl.CostEstimate(
            flops=work * HD * 4 * 2,
            bytes_accessed=n_home * NEW * QW * 8,
            transcendentals=work,
        ),
    )(segments, *named, *args)


def project_kernel(n_parts, core, *refs):
    w_ref, *outs = refs[max(n_parts, 1) :]
    if n_parts == 0:
        att = refs[0]
        keep_ref, send_ref = outs
    else:
        parts = refs[:n_parts]
        keep_ref, send_ref, att = outs

        @pl.when(pl.program_id(0) == 0)
        def _():
            merge(core, parts, att)

    result = jnp.dot(att[...], w_ref[...], preferred_element_type=F32).astype(BF)
    keep_ref[...] = result[: NEW // 2]
    send_ref[...] = result[NEW // 2 :]


def merge(core, parts, att):
    logs = []
    for part in parts:
        packed = part[:, QW:].astype(F32)
        logs.append(
            packed
            + pltpu.roll(packed, HD - GROUP, axis=1)
            + pltpu.roll(packed, HD - 2 * GROUP, axis=1)
        )
    top = functools.reduce(jnp.maximum, logs)
    shares = [jnp.exp(log - top) for log in logs]
    inverse = 1.0 / functools.reduce(jnp.add, shares)
    shares = [share * inverse for share in shares]
    for h in range(GROUP):
        cols = slice(h * HD, (h + 1) * HD)
        mixed = functools.reduce(
            jnp.add,
            [
                share[:, h : h + 1] * part[:, cols].astype(F32)
                for share, part in zip(shares, parts)
            ],
        ).astype(BF)
        for t in range(NEW // PIECE):
            away = jnp.where(core[0] == t % 2, 0, NEW // 2)
            at = pl.multiple_of(away + (t // 2) * PIECE, PIECE)
            att[pl.ds(at, PIECE), cols] = mixed[t * PIECE : (t + 1) * PIECE]


def project(core, parts, weight, column, columns):
    width = weight.shape[1] // columns
    tile = 1024
    steps = width // tile
    merged = len(parts) == 1
    half = pl.BlockSpec((NEW // 2, tile), lambda n, c: (0, n))
    att_spec = pl.BlockSpec((NEW, QW), lambda n, c: (0, 0))
    out_shape = [jax.ShapeDtypeStruct((NEW // 2, width), BF)] * 2
    out_specs = [half, half]
    if not merged:
        out_shape.append(jax.ShapeDtypeStruct((NEW, QW), BF))
        out_specs.append(att_spec)
    return pl.pallas_call(
        functools.partial(project_kernel, 0 if merged else len(parts)),
        out_shape=out_shape,
        grid_spec=pltpu.PrefetchScalarGridSpec(
            num_scalar_prefetch=1,
            grid=(steps,),
            in_specs=[pl.BlockSpec(part.shape, lambda n, c: (0, 0)) for part in parts]
            + [pl.BlockSpec((QW, tile), lambda n, c: (0, column * steps + n))],
            out_specs=out_specs,
        ),
        compiler_params=pltpu.CompilerParams(vmem_limit_bytes=63 << 20),
        cost_estimate=pl.CostEstimate(
            flops=4 * NEW * QW * width,
            bytes_accessed=QW * width * 2 + NEW * width * 2,
            transcendentals=0,
        ),
    )(core, *parts, weight)


def per_device(
    queries, new_keys, new_values, positions, cache_keys, cache_values, pattern, out_weight
):
    ctx = lax.axis_index("ctx")
    tp = lax.axis_index("tp")
    core = tp % 2
    x = tp // 2
    y, z = ctx // SIDE, ctx % SIDE

    places = digits(positions)
    picks = pattern.reshape(-1).astype(BF)
    q_own = jnp.concatenate([queries, jnp.pad(places.T, ((0, 0), (0, HD - 3)))], axis=1)
    q_meta = jnp.pad(picks, (0, META * SEND_W - picks.shape[0])).reshape(META, SEND_W)
    q_own = jnp.concatenate([q_own, q_meta], axis=0)
    k_meta = jnp.pad(places.reshape(-1, HD), ((0, META - 3 * NEW // HD), (0, 0)))
    kv_own = jnp.concatenate([cache_keys, new_keys, cache_values, new_values, k_meta], axis=0)

    order = (0, 1, 3, 2)
    q_at = {0: q_own}
    kv_at = {0: kv_own}
    for shift in (1, 3, 2):
        q_at[-shift % SIDE] = move(q_own, "q", shift)

    steps = jnp.array(order, jnp.int32)
    along_y = ((y + steps) % SIDE) * SIDE + z
    along_z = y * SIDE + (z + steps) % SIDE
    segments = jnp.where(core == 0, along_y, along_z)

    lengths = {1: 16, 3: 16, 2: 24}
    named = {o: q_at[o][NEW, :n].astype(jnp.int32) for o, n in lengths.items()}
    named[0] = pattern.reshape(-1)

    def run(homes, kvs, state=None, final=False, into=None, room=61):
        offsets = [order[n] for n in homes]
        return attend(
            segments,
            [named[o] for o in offsets],
            [q_at[o] for o in offsets],
            [kv_at[order[n]] for n in kvs],
            kvs[0],
            state,
            final,
            into,
            room,
        )

    own_state = run((0,), (0,), room=24)
    for shift in (1, 3):
        kv_at[-shift % SIDE] = move(kv_own, "k", shift)
    state = run((1, 2), (0,), into=(3, 0, None))
    state = run((3,), (0,), into=(3, 2, state))
    kv_at[2] = move(kv_own, "k", 2)
    state = run((1, 2, 3), (1, 2), state)
    partials = run((1, 2, 3), (3,), state, True)
    backs = [move(part, "q", order[n]) for n, part in zip((1, 2, 3), partials)]
    mine = run((0,), (1, 2, 3), own_state, True, room=24)

    core_id = core.reshape(1)
    keep0, send0, att = project(core_id, [*mine, *backs], out_weight, 0, 2)
    other0 = move(send0, "c", 0)
    keep1, send1 = project(core_id, [att], out_weight, 1, 2)
    other1 = move(send1, "c", 0)

    def finish(keep, other, way):
        def group(shift):
            at = ((x + shift) % XN) * PIECE
            return lax.dynamic_slice_in_dim(keep, at, PIECE, 0).astype(
                F32
            ) + lax.dynamic_slice_in_dim(other, at, PIECE, 0).astype(F32)

        back = -way % XN
        relay = move(group(2).astype(BF), "x", way)
        direct = move(group(back).astype(BF), "x", back)
        joined = (group(way) + relay.astype(F32)).astype(BF)
        joint = move(joined, "x", way)
        return (group(0) + direct.astype(F32) + joint.astype(F32)).astype(BF)

    return jnp.concatenate([finish(keep0, other0, 1), finish(keep1, other1, 3)], axis=1)


def solution(mesh):
    placed = (
        P("ctx", "tp"),
        P("ctx", "tp"),
        P("ctx", "tp"),
        P("ctx"),
        P("ctx", "tp"),
        P("ctx", "tp"),
        P("ctx", None),
        P("tp", None),
    )

    return jax.shard_map(
        per_device, mesh=mesh, in_specs=placed, out_specs=P(("ctx", "tp"), None), check_vma=False
    )
```

```python
import functools
import math

import jax
import jax.numpy as jnp
from jax import lax
from jax.experimental import pallas as pl
from jax.experimental.pallas import tpu as pltpu
from jax.sharding import PartitionSpec as P


HD = 128
GROUP = 8
SIDE = 4
XN = 4
QB = 64
PIECE = 32
STEP_ROWS = 256
STEP_KEYS = 512
SEG = 2048
NEW = 256
QW = GROUP * HD
META = 16
V_AT = SEG + NEW
RET_W = QW + 128
SEND_W = QW + 128
BASE = 64
NEG = -1e30
SCALE = 1.0 / math.sqrt(HD)
TO_EXP2 = SCALE * math.log2(math.e)
BF = jnp.bfloat16
F32 = jnp.float32
AXES = ("ctx", "tp")


def pairs(kind, shift):
    out = []
    for y in range(SIDE):
        for z in range(SIDE):
            for x in range(XN):
                for c in range(2):
                    to = [y, z, x, c]
                    if kind == "c":
                        to[3] = 1 - c
                    elif kind == "x":
                        to[2] = (x + shift) % XN
                    else:
                        along = (0 if c == 0 else 1) if kind == "k" else (1 if c == 0 else 0)
                        to[along] = (to[along] + shift) % SIDE
                    src = (y * SIDE + z) * 2 * XN + x * 2 + c
                    dst = (to[0] * SIDE + to[1]) * 2 * XN + to[2] * 2 + to[3]
                    out.append((src, dst))
    return out


def move(value, kind, shift):
    return lax.ppermute(value, AXES, pairs(kind, shift))


def digits(positions):
    p = positions.astype(jnp.int32)
    return jnp.stack([p // (BASE * BASE), (p // BASE) % BASE, p % BASE]).astype(BF)


def dot_t(a, b):
    return lax.dot_general(a, b, (((1,), (1,)), ((), ())), preferred_element_type=F32)


def attend_kernel(n_home, n_kv, first_kv, resume, final, *refs):
    refs = list(refs)
    flags = [refs.pop(0) for _ in range(n_home)]
    q_refs = [refs.pop(0) for _ in range(n_home)]
    kv_refs = [refs.pop(0) for _ in range(n_kv)]
    saved = [(refs.pop(0), refs.pop(0)) for _ in resume]
    if final:
        outs = [refs.pop(0) for _ in range(n_home)]
    else:
        acc_out, ml_out = refs[-10:-8]
    k_scr, v_scr, meta_scr, q_scr, qpos_scr, m_scr, acc_scr, sems = refs[-8:]
    home_id = pl.program_id(0)
    tokens = NEW
    blocks = NEW // QB

    def fetch(j):
        return (
            pltpu.make_async_copy(kv_refs[j].at[pl.ds(0, V_AT)], k_scr.at[j], sems.at[j, 0]),
            pltpu.make_async_copy(
                kv_refs[j].at[pl.ds(V_AT, V_AT)], v_scr.at[j, :, pl.ds(0, HD)], sems.at[j, 1]
            ),
            pltpu.make_async_copy(
                kv_refs[j].at[pl.ds(2 * V_AT, META)], meta_scr.at[j], sems.at[j, 2]
            ),
        )

    @pl.when(home_id == 0)
    def _():
        for j in range(n_kv):
            for copy in fetch(j):
                copy.start()
        for j in range(n_kv):
            v_scr[j, :, HD:] = jnp.ones((V_AT, HD), BF)

    if n_home == 1:
        q_src = q_refs[0]
    else:
        q_src = q_scr
        for home in range(n_home):

            @pl.when(home_id == home)
            def _(home=home):
                q_scr[...] = q_refs[home][...]

    def load(acc_in, ml_in):
        for h in range(GROUP):
            cols = slice(h * HD, (h + 1) * HD)
            m_scr[:, cols] = jnp.broadcast_to(ml_in[:, h : h + 1], (tokens, HD))
            acc_scr[:, h * 2 * HD : h * 2 * HD + HD] = acc_in[:, cols]
            acc_scr[:, h * 2 * HD + HD : (h + 1) * 2 * HD] = jnp.broadcast_to(
                ml_in[:, GROUP + h : GROUP + h + 1], (tokens, HD)
            )

    if not saved:
        m_scr[...] = jnp.full((tokens, QW), NEG, F32)
        acc_scr[...] = jnp.zeros((tokens, 2 * QW), F32)
    elif len(saved) == 1:
        load(*saved[0])
    else:
        start = 0
        for count, arrays in zip(resume, saved):
            inside = jnp.logical_and(home_id >= start, home_id < start + count)
            pl.when(inside)(functools.partial(load, *arrays))
            start += count

    @pl.when(home_id == 0)
    def _():
        for j in range(n_kv):
            for copy in fetch(j):
                copy.wait()

    packed = q_src[:, QW:].astype(F32)
    qpos_scr[...] = jnp.broadcast_to(
        packed[:, :1] * (BASE * BASE) + packed[:, 1:2] * BASE + packed[:, 2:3], (tokens, HD)
    )

    def advance(q, m, acc, k, v, mask):
        s = dot_t(q, k)
        if mask is not None:
            s = jnp.where(mask, s, NEG)
        peak = jnp.broadcast_to(jnp.max(s, axis=1, keepdims=True), m.shape)
        top = jnp.maximum(m, peak)
        p = jnp.exp2((s - jnp.concatenate([top] * (s.shape[1] // HD), axis=1)) * TO_EXP2)
        decay = jnp.exp2((m - top) * TO_EXP2)
        acc = acc * jnp.concatenate([decay, decay], axis=1) + jnp.dot(
            p.astype(BF), v, preferred_element_type=F32
        )
        return top, acc

    def fresh(j, carry):
        meta = meta_scr[j].astype(F32)
        parts = [
            jnp.concatenate([meta[2 * n : 2 * n + 1], meta[2 * n + 1 : 2 * n + 2]], axis=1)
            for n in range(3)
        ]
        kpos = parts[0] * (BASE * BASE) + parts[1] * BASE + parts[2]
        qpos = qpos_scr[...]
        mask = kpos <= jnp.concatenate([qpos, qpos], axis=1)
        k = k_scr[j, SEG:, :]
        v = v_scr[j, SEG:, :]
        for h in range(GROUP):
            cols = slice(h * HD, (h + 1) * HD)
            wide = slice(h * 2 * HD, (h + 1) * 2 * HD)
            top, acc = advance(q_src[:, cols], m_scr[:, cols], acc_scr[:, wide], k, v, mask)
            m_scr[:, cols] = top
            acc_scr[:, wide] = acc
        return carry

    per_pass = STEP_ROWS // QB

    def cached(item, carry):
        j, block = item // blocks, item % blocks
        at = (first_kv + j) * blocks + block
        hit = flags[0][at]
        for home in range(1, n_home):
            hit = jnp.where(home_id == home, flags[home][at], hit)

        @pl.when(hit > 0)
        def _():
            rows = pl.ds(pl.multiple_of(block * QB, QB), QB)
            for first in range(0, GROUP, per_pass):
                heads = range(first, first + per_pass)
                q = jnp.concatenate([q_src[rows, h * HD : (h + 1) * HD] for h in heads], axis=0)
                m = jnp.concatenate([m_scr[rows, h * HD : (h + 1) * HD] for h in heads], axis=0)
                acc = jnp.concatenate(
                    [acc_scr[rows, h * 2 * HD : (h + 1) * 2 * HD] for h in heads], axis=0
                )
                for n in range(SEG // STEP_KEYS):
                    keys = slice(n * STEP_KEYS, (n + 1) * STEP_KEYS)
                    m, acc = advance(q, m, acc, k_scr[j, keys, :], v_scr[j, keys, :], None)
                for n, h in enumerate(heads):
                    part = slice(n * QB, (n + 1) * QB)
                    m_scr[rows, h * HD : (h + 1) * HD] = m[part]
                    acc_scr[rows, h * 2 * HD : (h + 1) * 2 * HD] = acc[part]

        return carry

    if n_kv == 1:
        fresh(0, 0)
    else:
        lax.fori_loop(0, n_kv, fresh, 0)
    lax.fori_loop(0, n_kv * blocks, cached, 0)

    lane = lax.broadcasted_iota(jnp.int32, (tokens, HD), 1)
    if not final:
        ml = jnp.zeros((tokens, HD), F32)
        for h in range(GROUP):
            acc_out[:, h * HD : (h + 1) * HD] = acc_scr[:, h * 2 * HD : h * 2 * HD + HD]
            ml = jnp.where(lane == h, m_scr[:, h * HD : (h + 1) * HD], ml)
            ml = jnp.where(lane == GROUP + h, acc_scr[:, h * 2 * HD + HD : (h + 1) * 2 * HD], ml)
        ml_out[...] = ml
        return

    def emit(out):
        logs = jnp.zeros((tokens, HD), F32)
        for h in range(GROUP):
            cols = slice(h * HD, (h + 1) * HD)
            total = acc_scr[:, h * 2 * HD + HD : (h + 1) * 2 * HD]
            out[:, cols] = (acc_scr[:, h * 2 * HD : h * 2 * HD + HD] / total).astype(BF)
            log = m_scr[:, cols] * SCALE + jnp.log(total)
            logs = jnp.where(lax.rem(lane, GROUP) == h, log, logs)
        hi = logs.astype(BF).astype(F32)
        mid = (logs - hi).astype(BF).astype(F32)
        parts = jnp.where(lane < GROUP, hi, jnp.where(lane < 2 * GROUP, mid, logs - hi - mid))
        out[:, QW:] = parts.astype(BF)

    for home in range(n_home):
        if n_home == 1:
            emit(outs[0])
        else:
            pl.when(home_id == home)(functools.partial(emit, outs[home]))


def attend(flags, q_list, kv_list, first_kv, state=(), final=False):
    n_home, n_kv = len(q_list), len(kv_list)
    fixed = lambda shape: pl.BlockSpec(shape, lambda i, *f: (0,) * len(shape))
    turn = lambda width: pl.BlockSpec((NEW, width), lambda i, *f: (i, 0))
    in_specs = [fixed((NEW, SEND_W))] * n_home + [pl.BlockSpec(memory_space=pl.ANY)] * n_kv
    args = list(q_list) + list(kv_list)
    held, start = [], 0
    for pair in state:
        count = pair[0].shape[0] // NEW
        at = lambda i, *f, start=start, count=count: (jnp.clip(i - start, 0, count - 1), 0)
        in_specs += [pl.BlockSpec((NEW, QW), at), pl.BlockSpec((NEW, HD), at)]
        args += list(pair)
        held.append(count)
        start += count
    held = tuple(held)
    if final:
        out_shape = [jax.ShapeDtypeStruct((NEW, RET_W), BF)] * n_home
        out_specs = [fixed((NEW, RET_W))] * n_home
    else:
        out_shape = [
            jax.ShapeDtypeStruct((n_home * NEW, QW), F32),
            jax.ShapeDtypeStruct((n_home * NEW, HD), F32),
        ]
        out_specs = [turn(QW), turn(HD)]
    work = n_home * n_kv * NEW * GROUP * (SEG // 4 + NEW)
    return pl.pallas_call(
        functools.partial(attend_kernel, n_home, n_kv, first_kv, held, final),
        out_shape=out_shape,
        grid_spec=pltpu.PrefetchScalarGridSpec(
            num_scalar_prefetch=n_home,
            grid=(n_home,),
            in_specs=in_specs,
            out_specs=out_specs,
            scratch_shapes=[
                pltpu.VMEM((n_kv, V_AT, HD), BF),
                pltpu.VMEM((n_kv, V_AT, 2 * HD), BF),
                pltpu.VMEM((n_kv, META, HD), BF),
                pltpu.VMEM((NEW, SEND_W), BF),
                pltpu.VMEM((NEW, HD), F32),
                pltpu.VMEM((NEW, QW), F32),
                pltpu.VMEM((NEW, 2 * QW), F32),
                pltpu.SemaphoreType.DMA((n_kv, 3)),
            ],
        ),
        compiler_params=pltpu.CompilerParams(vmem_limit_bytes=24 << 20),
        cost_estimate=pl.CostEstimate(
            flops=work * HD * 4 * 2,
            bytes_accessed=n_home * NEW * QW * 8,
            transcendentals=work,
        ),
    )(*flags, *args)


def project_kernel(n_parts, core, *refs):
    w_ref, *outs = refs[max(n_parts, 1) :]
    if n_parts == 0:
        att = refs[0]
        keep_ref, send_ref = outs
    else:
        parts = refs[:n_parts]
        keep_ref, send_ref, att = outs

        @pl.when(pl.program_id(0) == 0)
        def _():
            merge(core, parts, att)

    result = jnp.dot(att[...], w_ref[...], preferred_element_type=F32).astype(BF)
    keep_ref[...] = result[: NEW // 2]
    send_ref[...] = result[NEW // 2 :]


def merge(core, parts, att):
    logs = []
    for part in parts:
        packed = part[:, QW:].astype(F32)
        logs.append(
            packed
            + pltpu.roll(packed, HD - GROUP, axis=1)
            + pltpu.roll(packed, HD - 2 * GROUP, axis=1)
        )
    top = functools.reduce(jnp.maximum, logs)
    shares = [jnp.exp(log - top) for log in logs]
    inverse = 1.0 / functools.reduce(jnp.add, shares)
    shares = [share * inverse for share in shares]
    for h in range(GROUP):
        cols = slice(h * HD, (h + 1) * HD)
        mixed = functools.reduce(
            jnp.add,
            [
                share[:, h : h + 1] * part[:, cols].astype(F32)
                for share, part in zip(shares, parts)
            ],
        ).astype(BF)
        for t in range(NEW // PIECE):
            away = jnp.where(core[0] == t % 2, 0, NEW // 2)
            at = pl.multiple_of(away + (t // 2) * PIECE, PIECE)
            att[pl.ds(at, PIECE), cols] = mixed[t * PIECE : (t + 1) * PIECE]


def project(core, parts, weight, column, columns):
    width = weight.shape[1] // columns
    tile = 1024
    steps = width // tile
    merged = len(parts) == 1
    half = pl.BlockSpec((NEW // 2, tile), lambda n, c: (0, n))
    att_spec = pl.BlockSpec((NEW, QW), lambda n, c: (0, 0))
    out_shape = [jax.ShapeDtypeStruct((NEW // 2, width), BF)] * 2
    out_specs = [half, half]
    if not merged:
        out_shape.append(jax.ShapeDtypeStruct((NEW, QW), BF))
        out_specs.append(att_spec)
    return pl.pallas_call(
        functools.partial(project_kernel, 0 if merged else len(parts)),
        out_shape=out_shape,
        grid_spec=pltpu.PrefetchScalarGridSpec(
            num_scalar_prefetch=1,
            grid=(steps,),
            in_specs=[pl.BlockSpec(part.shape, lambda n, c: (0, 0)) for part in parts]
            + [pl.BlockSpec((QW, tile), lambda n, c: (0, column * steps + n))],
            out_specs=out_specs,
        ),
        compiler_params=pltpu.CompilerParams(vmem_limit_bytes=24 << 20),
        cost_estimate=pl.CostEstimate(
            flops=4 * NEW * QW * width,
            bytes_accessed=QW * width * 2 + NEW * width * 2,
            transcendentals=0,
        ),
    )(core, *parts, weight)


def per_device(
    queries, new_keys, new_values, positions, cache_keys, cache_values, pattern, out_weight
):
    ctx = lax.axis_index("ctx")
    tp = lax.axis_index("tp")
    core = tp % 2
    x = tp // 2
    y, z = ctx // SIDE, ctx % SIDE

    places = digits(positions)
    picks = pattern.reshape(-1).astype(BF)
    q_own = jnp.concatenate([queries, jnp.pad(places.T, ((0, 0), (0, HD - 3)))], axis=1)
    q_meta = jnp.pad(picks, (0, META * SEND_W - picks.shape[0])).reshape(META, SEND_W)
    q_own = jnp.concatenate([q_own, q_meta], axis=0)
    k_meta = jnp.pad(places.reshape(-1, HD), ((0, META - 3 * NEW // HD), (0, 0)))
    kv_own = jnp.concatenate([cache_keys, new_keys, cache_values, new_values, k_meta], axis=0)

    order = (0, 1, 3, 2)
    q_at = {0: q_own}
    kv_at = {0: kv_own}
    for shift in (1, 3, 2):
        q_at[-shift % SIDE] = move(q_own, "q", shift)

    steps = jnp.array(order, jnp.int32)
    along_y = ((y + steps) % SIDE) * SIDE + z
    along_z = y * SIDE + (z + steps) % SIDE
    segments = jnp.where(core == 0, along_y, along_z).astype(F32)

    def flags_of(row):
        named = row.astype(F32).reshape(1, NEW // QB, -1)
        hits = named == segments[:, None, None]
        return jnp.sum(hits.astype(jnp.int32), axis=-1).reshape(-1)

    flags = {0: flags_of(picks)}

    def read_flags(offsets, done):
        for o in offsets:
            row = q_at[o][NEW, : picks.shape[0]]
            flags[o] = flags_of(lax.optimization_barrier((row, *done))[0])

    def run(homes, kvs, state=(), final=False):
        offsets = [order[n] for n in homes]
        return attend(
            [flags[o] for o in offsets],
            [q_at[o] for o in offsets],
            [kv_at[order[n]] for n in kvs],
            kvs[0],
            state,
            final,
        )

    own_state = run((0,), (0,))
    for shift in (1, 3):
        kv_at[-shift % SIDE] = move(kv_own, "k", shift)
    read_flags((1, 3), own_state)
    close = run((1, 2), (0,))
    read_flags((2,), close)
    distant = run((3,), (0,))
    kv_at[2] = move(kv_own, "k", 2)
    state = run((1, 2, 3), (1, 2), [close, distant])
    partials = run((1, 2, 3), (3,), [state], True)
    backs = [move(part, "q", order[n]) for n, part in zip((1, 2, 3), partials)]
    mine = run((0,), (1, 2, 3), [own_state], True)

    core_id = core.reshape(1)
    keep0, send0, att = project(core_id, [*mine, *backs], out_weight, 0, 2)
    other0 = move(send0, "c", 0)
    keep1, send1 = project(core_id, [att], out_weight, 1, 2)
    other1 = move(send1, "c", 0)

    def finish(keep, other, way):
        def group(shift):
            at = ((x + shift) % XN) * PIECE
            return lax.dynamic_slice_in_dim(keep, at, PIECE, 0).astype(
                F32
            ) + lax.dynamic_slice_in_dim(other, at, PIECE, 0).astype(F32)

        back = -way % XN
        relay = move(group(2).astype(BF), "x", way)
        direct = move(group(back).astype(BF), "x", back)
        joined = (group(way) + relay.astype(F32)).astype(BF)
        joint = move(joined, "x", way)
        return (group(0) + direct.astype(F32) + joint.astype(F32)).astype(BF)

    return jnp.concatenate([finish(keep0, other0, 1), finish(keep1, other1, 3)], axis=1)


def solution(mesh):
    placed = (
        P("ctx", "tp"),
        P("ctx", "tp"),
        P("ctx", "tp"),
        P("ctx"),
        P("ctx", "tp"),
        P("ctx", "tp"),
        P("ctx", None),
        P("tp", None),
    )

    return jax.shard_map(
        per_device, mesh=mesh, in_specs=placed, out_specs=P(("ctx", "tp"), None), check_vma=False
    )
```
